128 devices in a mesh: gx: 32 (over y_hi, x, z), gy: 4 (over y_lo, core).
Axes of the slice: x: 4, y: 4 (y_hi: 2, y_lo: 2; y = y_hi * 2 + y_lo), z: 4, core: 2. Of those that a mesh axis runs over, the one named last changes fastest.
Arguments:
- volume: bfloat16 [16, 128, 32, 256], P(None, 'gx', 'gy'), may hold values from -6 to 6
- fine_kernel: bfloat16 [3, 3, 3, 16, 16], replicated, may hold values from -0.3125 to 0.3125
- coarse_kernel: bfloat16 [3, 3, 3, 32, 16], replicated, may hold values from -0.3125 to 0.3125
- fine_cotangent: bfloat16 [16, 128, 32, 256], P(None, 'gx', 'gy'), may hold values from -6 to 6
- coarse_cotangent: bfloat16 [32, 64, 16, 128], P(None, 'gx', 'gy'), may hold values from -18 to 18
Outputs:
- fine_out: bfloat16 [16, 128, 32, 256], P(None, 'gx', 'gy')
- coarse_out: bfloat16 [32, 64, 16, 128], P(None, 'gx', 'gy')
- volume_grad: bfloat16 [16, 128, 32, 256], P(None, 'gx', 'gy')
- fine_kernel_grad: float32 [3, 3, 3, 16, 16], replicated
- coarse_kernel_grad: float32 [3, 3, 3, 32, 16], replicated
The draws below stay inside these ranges and needn't reach their ends.
All inputs are finite; a program needn't handle non-finite values.
Results may differ from the reference program's by a relative error of at most 0.0064.
Values may be sent and summed in bfloat16 or wider, within the bound.
A program may use at most 64 MiB of HBM per device.

```python
import jax
import jax.numpy as jnp
from jax import lax

C1 = 16
C2 = 32
NZ = 128
NY = 32
NX = 256


def steps_of(key, extent, pieces, low, high):
    gain, own = 1.0, jax.random.fold_in(key, 6)
    for axis_at, shards_of in pieces:
        steps = jnp.exp(jax.random.uniform(jax.random.fold_in(own, axis_at), (shards_of,), jnp.float32, low / len(pieces), high / len(pieces)))
        gain = gain * jnp.repeat(steps, extent[axis_at] // shards_of).reshape([-1 if axis == axis_at else 1 for axis in range(len(extent))])
    return gain


def centred(own_key, extent, width, bound, split=(), kind=jnp.bfloat16):
    entries = jax.random.normal(own_key, extent, jnp.float32) * width
    if len(split) > 0:
        entries = steps_of(own_key, extent, split, -0.22, 0.18) * entries
    return jnp.clip(entries, min=-bound, max=bound).astype(kind)


def setup_inputs(seed: int = 0) -> dict:
    seeds = jax.random.split(jax.random.key(seed), 6)
    return {
        "volume": centred(seeds[0], (C1, NZ, NY, NX), 1.0, 6.0, ((1, 32), (2, 4))),
        "fine_kernel": centred(seeds[1], (3, 3, 3, C1, C1), (27 * C1) ** -0.5, 0.3125),
        "coarse_kernel": centred(seeds[2], (3, 3, 3, C2, C1), (27 * C1) ** -0.5, 0.3125),
        "fine_cotangent": centred(seeds[3], (C1, NZ, NY, NX), 1.0, 6.0, ((1, 32), (2, 4))),
        "coarse_cotangent": centred(seeds[4], (C2, NZ // 2, NY // 2, NX // 2), 3.0, 18.0, ((1, 32), (2, 4))),
    }


def silu_slope(values):
    sigma = jax.nn.sigmoid(values)
    return sigma * (1.0 + values * (1.0 - sigma))


def pad_cells(values):
    return jnp.pad(values, ((0, 0), (1, 1), (1, 1), (1, 1)))


def correlate(padded, weights, flipped, depth_cells, row_count, width_cells):
    summed = None
    for shift_z in range(3):
        for shift_y in range(3):
            for shift_x in range(3):
                if flipped:
                    matrix = weights[shift_z, shift_y, shift_x].T
                    start_z, start_y, start_x = 2 - shift_z, 2 - shift_y, 2 - shift_x
                else:
                    matrix = weights[shift_z, shift_y, shift_x]
                    start_z, start_y, start_x = shift_z, shift_y, shift_x
                piece = padded[:, start_z:start_z + depth_cells, start_y:start_y + row_count, start_x:start_x + width_cells]
                piece = piece.reshape(padded.shape[0], -1)
                contrib = jnp.dot(matrix, piece, preferred_element_type=jnp.float32)
                summed = contrib if summed is None else summed + contrib
    return summed.reshape(-1, depth_cells, row_count, width_cells)


def kernel_terms(slope, padded):
    depth_cells, row_count, width_cells = slope.shape[1:]
    flat_slope = slope.reshape(slope.shape[0], -1)
    stacked = []
    for shift_z in range(3):
        for shift_y in range(3):
            for shift_x in range(3):
                piece = padded[:, shift_z:shift_z + depth_cells, shift_y:shift_y + row_count, shift_x:shift_x + width_cells]
                piece = piece.reshape(padded.shape[0], -1)
                stacked.append(lax.dot_general(flat_slope, piece, (((1,), (1,)), ((), ())), preferred_element_type=jnp.float32))
    return jnp.stack(stacked).reshape(3, 3, 3, slope.shape[0], padded.shape[0])


def pool_mean(values):
    chans, depth_cells, row_count, width_cells = values.shape
    blocks = values.astype(jnp.float32).reshape(chans, depth_cells // 2, 2, row_count // 2, 2, width_cells // 2, 2)
    return blocks.mean(axis=(2, 4, 6))


def spread_cells(grads):
    chans, depth_cells, row_count, width_cells = grads.shape
    wide = jnp.broadcast_to(grads[:, :, None, :, None, :, None], (chans, depth_cells, 2, row_count, 2, width_cells, 2))
    return wide.reshape(chans, 2 * depth_cells, 2 * row_count, 2 * width_cells) / 8.0


def reference(volume, fine_kernel, coarse_kernel, fine_cotangent, coarse_cotangent):
    fine_shape = volume.shape[1:]
    padded = pad_cells(volume)
    fine_pre = correlate(padded, fine_kernel, False, *fine_shape)
    fine_out = (volume.astype(jnp.float32) + jax.nn.silu(fine_pre)).astype(jnp.bfloat16)
    pooled = pool_mean(fine_out).astype(jnp.bfloat16)
    coarse_shape = pooled.shape[1:]
    pooled_pad = pad_cells(pooled)
    coarse_pre = correlate(pooled_pad, coarse_kernel, False, *coarse_shape)
    coarse_out = jax.nn.silu(coarse_pre).astype(jnp.bfloat16)
    coarse_slope = (coarse_cotangent.astype(jnp.float32) * silu_slope(coarse_pre)).astype(jnp.bfloat16)
    pooled_grad = correlate(pad_cells(coarse_slope), coarse_kernel, True, *coarse_shape)
    fine_grad = fine_cotangent.astype(jnp.float32) + spread_cells(pooled_grad)
    fine_slope = (fine_grad * silu_slope(fine_pre)).astype(jnp.bfloat16)
    volume_grad = (fine_grad + correlate(pad_cells(fine_slope), fine_kernel, True, *fine_shape)).astype(jnp.bfloat16)
    fine_kernel_grad = kernel_terms(fine_slope, padded) * (NZ * NY * NX) ** -0.5
    coarse_kernel_grad = kernel_terms(coarse_slope, pooled_pad) * (NZ * NY * NX // 8) ** -0.5
    return fine_out, coarse_out, volume_grad, fine_kernel_grad, coarse_kernel_grad
```

```python
import jax
import jax.numpy as jnp
from jax import lax
from jax.experimental import pallas as pl
from jax.experimental.pallas import tpu as pltpu
from jax.sharding import PartitionSpec as P

F32 = jnp.float32
BF16 = jnp.bfloat16
MESH = pl.DeviceIdType.MESH
C1, C2 = 16, 32
D, R, W = 4, 8, 256
HD, HR, HW = 2, 4, 128
NGX, NGY = 32, 4
DIRS = [(sx, sy) for sx in (-1, 0, 1) for sy in (-1, 0, 1) if (sx, sy) != (0, 0)]
NT = (((1,), (1,)), ((), ()))


def dot(a, b):
    return jnp.dot(a, b, preferred_element_type=F32)


def dot_nt(a, b):
    return lax.dot_general(a, b, NT, preferred_element_type=F32)


def shifted(x):
    n = x.shape[1]
    lane = lax.broadcasted_iota(jnp.int32, x.shape, 1)
    before = jnp.where(lane == 0, 0.0, pltpu.roll(x, 1, axis=1))
    after = jnp.where(lane == n - 1, 0.0, pltpu.roll(x, n - 1, axis=1))
    return before.astype(BF16), after.astype(BF16)


def exists(gx, gy, sx, sy):
    cond = None
    for ok in (
        [gx < NGX - 1] if sx == 1 else [gx > 0] if sx == -1 else []
    ) + ([gy < NGY - 1] if sy == 1 else [gy > 0] if sy == -1 else []):
        cond = ok if cond is None else jnp.logical_and(cond, ok)
    return cond


def span(s, h, n, sending):
    if s == 0:
        return h, n
    if sending:
        return (n, h) if s == 1 else (h, h)
    return (0, h) if s == 1 else (h + n, h)


class Halo:
    def __init__(self, buf, chan, h, nz, ny, send_sem, recv_sem, gx, gy):
        self.buf, self.chan, self.h, self.nz, self.ny = buf, chan, h, nz, ny
        self.send_sem, self.recv_sem, self.gx, self.gy = send_sem, recv_sem, gx, gy

    def part(self, sx, sy, sending):
        z0, zn = span(sx, self.h, self.nz, sending)
        y0, yn = span(sy, self.h, self.ny, sending)
        return self.buf.at[pl.ds(z0, zn), pl.ds(y0, yn), self.chan, :]

    def desc(self, i):
        sx, sy = DIRS[i]
        return pltpu.make_async_remote_copy(
            src_ref=self.part(sx, sy, True),
            dst_ref=self.part(sx, sy, False),
            send_sem=self.send_sem.at[i],
            recv_sem=self.recv_sem.at[i],
            device_id=(self.gx + sx, self.gy + sy),
            device_id_type=MESH,
        )

    def clear_edges(self):
        h, nz, ny = self.h, self.nz, self.ny
        for s, n, axis, g, last in (
            (-1, nz, 0, self.gx, 0),
            (1, nz, 0, self.gx, NGX - 1),
            (-1, ny, 1, self.gy, 0),
            (1, ny, 1, self.gy, NGY - 1),
        ):
            at = 0 if s == -1 else h + n
            rows = pl.ds(at, h)

            @pl.when(g == last)
            def _(axis=axis, rows=rows):
                index = (rows, slice(None)) if axis == 0 else (slice(None), rows)
                view = self.buf.at[(*index, self.chan, slice(None))]
                view[...] = jnp.zeros(view.shape, view.dtype)

    def start(self):
        for i, (sx, sy) in enumerate(DIRS):

            @pl.when(exists(self.gx, self.gy, sx, sy))
            def _(i=i):
                self.desc(i).start()

    def wait_recv(self):
        for i, (sx, sy) in enumerate(DIRS):

            @pl.when(exists(self.gx, self.gy, -sx, -sy))
            def _(i=i):
                self.desc(i).wait_recv()

    def wait_send(self):
        for i, (sx, sy) in enumerate(DIRS):

            @pl.when(exists(self.gx, self.gy, sx, sy))
            def _(i=i):
                self.desc(i).wait_send()


class AllReduce:
    def __init__(self, terms, rs, bx, fin, sems, na, nb, a, b, dev_a, dev_b):
        self.terms, self.rs, self.bx, self.fin = terms, rs, bx, fin
        self.na, self.nb, self.a, self.b = na, nb, a, b
        self.dev_a, self.dev_b = dev_a, dev_b
        self.rs_s, self.rs_r, self.b_s, self.b_r, self.g_s, self.g_r = sems

    def rs_copy(self, k):
        d = lax.rem(self.a + k, self.na)
        return pltpu.make_async_remote_copy(
            self.terms.at[d], self.rs.at[k], self.rs_s.at[k], self.rs_r.at[k], self.dev_a(d), MESH
        )

    def b_copy(self, k):
        d = lax.rem(self.b + k, self.nb)
        return pltpu.make_async_remote_copy(
            self.bx.at[self.b], self.bx.at[self.b], self.b_s.at[k], self.b_r.at[k], self.dev_b(d), MESH
        )

    def g_copy(self, k):
        d = lax.rem(self.a + k, self.na)
        return pltpu.make_async_remote_copy(
            self.fin.at[self.a], self.fin.at[self.a], self.g_s.at[k], self.g_r.at[k], self.dev_a(d), MESH
        )

    def start_scatter(self):
        for k in range(1, self.na):
            self.rs_copy(k).start()

    def start_exchange(self):
        total = self.terms[self.a]
        for k in range(1, self.na):
            self.rs_copy(k).wait_recv()
        for k in range(1, self.na):
            total = total + self.rs[k]
        self.bx[self.b] = total
        for k in range(1, self.nb):
            self.b_copy(k).start()

    def start_gather(self):
        for k in range(1, self.nb):
            self.b_copy(k).wait_recv()
        total = self.bx[0]
        for k in range(1, self.nb):
            total = total + self.bx[k]
        self.fin[self.a] = total
        for k in range(1, self.na):
            self.g_copy(k).start()

    def finish(self):
        for k in range(1, self.na):
            self.g_copy(k).wait_recv()

    def wait_send(self):
        for k in range(1, self.na):
            self.rs_copy(k).wait_send()
            self.g_copy(k).wait_send()
        for k in range(1, self.nb):
            self.b_copy(k).wait_send()


def kernel(
    vol_hbm, fcot_hbm, ccot_hbm, wf_ref, kf_ref, wc_ref, kc_ref,
    fo_ref, co_ref, vg_ref, fk_ref, ck_ref,
    raw_v, raw_f, raw_c, st_v, st_f, st_c, st_o, st_co,
    vp, cp, qp, tp, sp, fob, g1, fg, csb, wft, wct, ft, ct,
    frs, fbx, ffin, crs, cbx, cfin,
    in_sem, hs, hr, f_rs_s, f_rs_r, f_b_s, f_b_r, f_g_s, f_g_r,
    c_rs_s, c_rs_r, c_b_s, c_b_r, c_g_s, c_g_r,
):
    gx, gy = lax.axis_index("gx"), lax.axis_index("gy")
    mid = pl.ds(C1, C1)
    loads = [
        pltpu.make_async_copy(src, dst, in_sem.at[i])
        for i, (src, dst) in enumerate(
            ((vol_hbm, raw_v), (ccot_hbm, raw_c), (fcot_hbm, raw_f))
        )
    ]
    for load in loads:
        load.start()

    zi, hi = lax.rem(gx, 4), lax.div(gx, 4)
    y_lo, core = lax.div(gy, 2), lax.rem(gy, 2)
    base = hi * 4

    def c_dev_a(d):
        return (base + lax.div(d, 4), lax.rem(d, 4))

    def c_dev_b(d):
        return (d * 4 + zi, gy)

    def f_dev_a(d):
        return (base + lax.div(d, 2), lax.rem(d, 2) * 2 + core)

    def f_dev_b(d):
        return (lax.div(d, 2) * 4 + zi, y_lo * 2 + lax.rem(d, 2))

    barrier = pltpu.get_barrier_semaphore()

    def greet(device):
        pl.semaphore_signal(barrier, inc=1, device_id=device, device_id_type=MESH)

    for sx, sy in DIRS:

        @pl.when(exists(gx, gy, sx, sy))
        def _(sx=sx, sy=sy):
            greet((gx + sx, gy + sy))

    a_c, a_f, b_f = zi * 4 + gy, zi * 2 + y_lo, hi * 2 + core
    for k in range(1, 16):
        greet(c_dev_a(lax.rem(a_c + k, 16)))
        greet(f_dev_b(lax.rem(b_f + k, 16)))

    vhalo = Halo(vp, mid, 1, D, R, hs.at[0], hr.at[0], gx, gy)
    chalo = Halo(cp, slice(None), 1, HD, HR, hs.at[1], hr.at[1], gx, gy)
    qhalo = Halo(qp, mid, 2, HD, HR, hs.at[2], hr.at[2], gx, gy)
    shalo = Halo(sp, mid, 1, D, R, hs.at[3], hr.at[3], gx, gy)
    f_sum = AllReduce(
        ft, frs, fbx, ffin, (f_rs_s, f_rs_r, f_b_s, f_b_r, f_g_s, f_g_r),
        8, 16, a_f, b_f, f_dev_a, f_dev_b,
    )
    c_sum = AllReduce(
        ct, crs, cbx, cfin, (c_rs_s, c_rs_r, c_b_s, c_b_r, c_g_s, c_g_r),
        16, 8, a_c, hi, c_dev_a, c_dev_b,
    )

    eye1 = (
        lax.broadcasted_iota(jnp.int32, (C1, C1), 0) == lax.broadcasted_iota(jnp.int32, (C1, C1), 1)
    ).astype(F32).astype(BF16)
    wft[...] = dot_nt(eye1, kf_ref[...]).astype(BF16)
    wct[...] = dot_nt(eye1, kc_ref[...]).astype(BF16)
    for halo in (vhalo, chalo, qhalo, shalo):
        halo.clear_edges()

    loads[0].wait()
    for t in range(2):
        st_v[t] = raw_v[:, t * 128 : (t + 1) * 128].astype(F32)
    for z in range(D):
        for y in range(R):
            for t in range(2):
                vp[z + 1, y + 1, mid, pl.ds(t * 128, 128)] = st_v[
                    t, pl.ds(z * R + y, C1, stride=D * R), :
                ].astype(BF16)
    loads[1].wait()
    st_c[...] = raw_c[...].astype(F32)
    for z in range(HD):
        for y in range(HR):
            cp[z + 1, y + 1] = st_c[pl.ds(z * HR + y, C2, stride=HD * HR), :].astype(BF16)
    n_halo = 0
    for sx, sy in DIRS:
        n_halo = n_halo + exists(gx, gy, sx, sy).astype(jnp.int32)
    pl.semaphore_wait(barrier, n_halo + 30)
    vhalo.start()
    chalo.start()

    def put_shifts(buf, z, y, order):
        before, after = shifted(buf[z, y, mid, :].astype(F32))
        low, high = (before, after) if order > 0 else (after, before)
        buf[z, y, pl.ds(0, C1), :] = low
        buf[z, y, pl.ds(2 * C1, C1), :] = high

    def own_shifts(buf, h, nz, ny, order):
        @pl.loop(0, nz)
        def _(z):
            for y in range(ny):
                put_shifts(buf, z + h, y + h, order)

    def halo_shifts(buf, h, nz, ny, order):
        @pl.loop(0, h)
        def _(z):
            for y in range(ny + 2 * h):
                put_shifts(buf, z, y, order)
                put_shifts(buf, z + h + nz, y, order)

        @pl.loop(0, nz)
        def _(z):
            for y in range(h):
                put_shifts(buf, z + h, y, order)
                put_shifts(buf, z + h, y + h + ny, order)

    def taps(buf, z, y, back=False):
        rows = []
        for a in range(3):
            for b in range(3):
                da, db = (2 - a, 2 - b) if back else (a, b)
                rows.append(buf[z + da, y + db])
        return jnp.concatenate(rows, axis=0)

    own_shifts(vp, 1, D, R, 1)
    loads[2].wait()
    for t in range(2):
        st_f[t] = raw_f[:, t * 128 : (t + 1) * 128].astype(F32)
    pool_row = lax.broadcasted_iota(jnp.int32, (W, HW), 0)
    pool_col = lax.broadcasted_iota(jnp.int32, (W, HW), 1)
    pool_mat = (lax.div(pool_row, 2) == pool_col).astype(F32).astype(BF16)
    vhalo.wait_recv()
    halo_shifts(vp, 1, D, R, 1)
    wf = wf_ref[...]

    @pl.loop(0, HD)
    def _(zc):
        for zz in range(2):
            z = zc * 2 + zz
            for y in range(R):
                pre = dot(wf, taps(vp, z, y))
                s = jax.nn.sigmoid(pre)
                out = (vp[z + 1, y + 1, mid, :].astype(F32) + pre * s).astype(BF16)
                g1[z, y] = s * (1.0 + pre * (1.0 - s))
                fob[z, y] = out
                out = out.astype(F32)
                for t in range(2):
                    st_o[t, pl.ds(z * R + y, C1, stride=D * R), :] = out[:, t * 128 : (t + 1) * 128]
        for yc in range(HR):
            four = fob[pl.ds(zc * 2, 2), pl.ds(yc * 2, 2)].reshape(4 * C1, W)
            half = dot(four, pool_mat)
            total = half[0:16] + half[16:32] + half[32:48] + half[48:64]
            qp[zc + 2, yc + 2, mid, :] = (total * 0.125).astype(BF16)

    qhalo.start()
    for t in range(2):
        fo_ref[:, t * 128 : (t + 1) * 128] = st_o[t].astype(BF16)
    own_shifts(qp, 2, HD, HR, 1)
    up_row = lax.broadcasted_iota(jnp.int32, (HW, 3 * W), 0)
    up_col = lax.broadcasted_iota(jnp.int32, (HW, 3 * W), 1)
    up_mat = (
        up_row == lax.div(lax.rem(up_col, W), 2) + 1 - lax.div(up_col, W)
    ).astype(F32).astype(BF16)
    wc = wc_ref[...]
    chalo.wait_recv()
    qhalo.wait_recv()
    halo_shifts(qp, 2, HD, HR, 1)

    @pl.loop(0, HD + 2)
    def _(z):
        for y in range(HR + 2):
            pre = dot(wc, taps(qp, z, y))
            s = jax.nn.sigmoid(pre)
            slope = cp[z, y].astype(F32) * (s * (1.0 + pre * (1.0 - s)))
            csb[z, y] = slope.astype(BF16)
            if 1 <= y <= HR:

                @pl.when(jnp.logical_and(z >= 1, z <= HD))
                def _(y=y, pre=pre, s=s):
                    st_co[pl.ds((z - 1) * HR + y - 1, C2, stride=HD * HR), :] = (
                        (pre * s).astype(BF16).astype(F32)
                    )
        wide = dot(csb[z].reshape((HR + 2) * C2, HW), up_mat).astype(BF16)
        for c in range(3):
            tp[z, :, pl.ds(c * C2, C2), :] = wide[:, c * W : (c + 1) * W].reshape(HR + 2, C2, W)

    co_ref[...] = st_co[...].astype(BF16)

    ck = jnp.zeros((C2, 27 * C1), F32)
    for z in range(HD):
        for y in range(HR):
            ck = ck + dot_nt(csb[z + 1, y + 1], taps(qp, z + 1, y + 1))
    ck = jnp.concatenate([ck, jnp.zeros((C2, 80), F32)], axis=1)
    for i in range(4):
        for t in range(4):
            ct[i * 4 + t] = ck[i * 8 : (i + 1) * 8, t * 128 : (t + 1) * 128]
    c_sum.start_scatter()

    wct_v = wct[...]

    @pl.loop(0, HD)
    def _(zc):
        for yc in range(HR):
            spread = dot(wct_v, taps(tp, zc, yc, True)) * 0.125
            for zz in range(2):
                for yy in range(2):
                    z, y = zc * 2 + zz, yc * 2 + yy
                    cot = jnp.concatenate(
                        [st_f[t, pl.ds(z * R + y, C1, stride=D * R), :] for t in range(2)], axis=1
                    )
                    grad = cot + spread
                    fg[z, y] = grad
                    sp[z + 1, y + 1, mid, :] = (grad * g1[z, y]).astype(BF16)

    shalo.start()
    c_sum.start_exchange()

    def fine_terms(z, acc):
        for y in range(R):
            acc = acc + dot_nt(sp[z + 1, y + 1, mid, :], taps(vp, z, y))
        return acc

    fk = lax.fori_loop(0, D, fine_terms, jnp.zeros((C1, 27 * C1), F32))
    fk = jnp.concatenate([fk, jnp.zeros((C1, 80), F32)], axis=1)
    for i in range(2):
        for t in range(4):
            ft[i * 4 + t] = fk[i * 8 : (i + 1) * 8, t * 128 : (t + 1) * 128]
    f_sum.start_scatter()
    c_sum.start_gather()
    own_shifts(sp, 1, D, R, -1)
    f_sum.start_exchange()
    shalo.wait_recv()
    halo_shifts(sp, 1, D, R, -1)
    wft_v = wft[...]

    def volume_rows(z):
        for y in range(R):
            total = fg[z, y] + dot(wft_v, taps(sp, z, y, True))
            for t in range(2):
                st_o[t, pl.ds(z * R + y, C1, stride=D * R), :] = total[:, t * 128 : (t + 1) * 128]

    @pl.loop(0, HD)
    def _(z):
        volume_rows(z)

    f_sum.start_gather()

    @pl.loop(HD, D)
    def _(z):
        volume_rows(z)

    for t in range(2):
        vg_ref[:, t * 128 : (t + 1) * 128] = st_o[t].astype(BF16)

    def emit(fin, out, rows, scale):
        for i in range(rows):
            for t in range(4):
                tile = fin[i * 4 + t] * scale
                for k in range(8):
                    tap = t * 8 + k
                    if tap < 27:
                        out[tap, pl.ds(i * 8, 8), :] = tile[:, k * C1 : (k + 1) * C1]

    c_sum.finish()
    emit(cfin, ck_ref, 4, 131072.0**-0.5)
    f_sum.finish()
    emit(ffin, fk_ref, 2, 1048576.0**-0.5)
    for one in (vhalo, chalo, qhalo, shalo, c_sum, f_sum):
        one.wait_send()


def local(volume, fine_kernel, coarse_kernel, fine_cotangent, coarse_cotangent):
    wf = fine_kernel.transpose(3, 0, 1, 2, 4).reshape(C1, 27 * C1)
    wc = coarse_kernel.transpose(3, 0, 1, 2, 4).reshape(C2, 27 * C1)
    kf = fine_kernel.reshape(27 * C1, C1)
    kc = coarse_kernel.reshape(27 * C2, C1)
    any_spec = pl.BlockSpec(memory_space=pl.ANY)
    vmem = pl.BlockSpec(memory_space=pltpu.VMEM)
    dma = pltpu.SemaphoreType.DMA
    V = pltpu.VMEM
    tile = (8, 128)
    outs = pl.pallas_call(
        kernel,
        out_shape=[
            jax.ShapeDtypeStruct((C1 * D * R, W), BF16),
            jax.ShapeDtypeStruct((C2 * HD * HR, HW), BF16),
            jax.ShapeDtypeStruct((C1 * D * R, W), BF16),
            jax.ShapeDtypeStruct((27, C1, C1), F32),
            jax.ShapeDtypeStruct((27, C2, C1), F32),
        ],
        in_specs=[any_spec] * 3 + [vmem] * 4,
        out_specs=[vmem] * 5,
        scratch_shapes=[
            V((C1 * D * R, W), BF16), V((C1 * D * R, W), BF16), V((C2 * HD * HR, HW), BF16),
            V((2, C1 * D * R, 128), F32), V((2, C1 * D * R, 128), F32), V((C2 * HD * HR, HW), F32),
            V((2, C1 * D * R, 128), F32), V((C2 * HD * HR, HW), F32),
            V((D + 2, R + 2, 3 * C1, W), BF16),
            V((HD + 2, HR + 2, C2, HW), BF16),
            V((HD + 4, HR + 4, 3 * C1, HW), BF16),
            V((HD + 2, HR + 2, 3 * C2, W), BF16),
            V((D + 2, R + 2, 3 * C1, W), BF16),
            V((D, R, C1, W), BF16), V((D, R, C1, W), F32), V((D, R, C1, W), F32),
            V((HD + 2, HR + 2, C2, HW), BF16),
            V((C1, 27 * C1), BF16), V((C1, 27 * C2), BF16),
            V((8, *tile), F32), V((16, *tile), F32),
            V((8, *tile), F32), V((16, *tile), F32), V((8, *tile), F32),
            V((16, *tile), F32), V((8, *tile), F32), V((16, *tile), F32),
            dma((3,)), dma((4, 8)), dma((4, 8)),
            dma((8,)), dma((8,)), dma((16,)), dma((16,)), dma((8,)), dma((8,)),
            dma((16,)), dma((16,)), dma((8,)), dma((8,)), dma((16,)), dma((16,)),
        ],
        compiler_params=pltpu.CompilerParams(
            collective_id=0, has_side_effects=True, vmem_limit_bytes=48 << 20
        ),
        name="unet_levels",
    )(
        volume.reshape(C1 * D * R, W),
        fine_cotangent.reshape(C1 * D * R, W),
        coarse_cotangent.reshape(C2 * HD * HR, HW),
        wf, kf, wc, kc,
    )
    fo, co, vg, fk, ck = outs
    return (
        fo.reshape(volume.shape),
        co.reshape(coarse_cotangent.shape),
        vg.reshape(volume.shape),
        fk.reshape(fine_kernel.shape),
        ck.reshape(coarse_kernel.shape),
    )


def solution(mesh):
    block = P(None, "gx", "gy", None)
    return jax.shard_map(
        local,
        mesh=mesh,
        in_specs=(block, P(), P(), block, block),
        out_specs=(block, block, block, P(), P()),
        check_vma=False,
    )
```

```python
import jax
import jax.numpy as jnp
from jax import lax
from jax.experimental import pallas as pl
from jax.experimental.pallas import tpu as pltpu
from jax.sharding import PartitionSpec as P

F32 = jnp.float32
BF16 = jnp.bfloat16
MESH = pl.DeviceIdType.MESH
C1, C2 = 16, 32
D, R, W = 4, 8, 256
HD, HR, HW = 2, 4, 128
NGX, NGY = 32, 4
DIRS = [(sx, sy) for sx in (-1, 0, 1) for sy in (-1, 0, 1) if (sx, sy) != (0, 0)]
NT = (((1,), (1,)), ((), ()))


def dot(a, b):
    return jnp.dot(a, b, preferred_element_type=F32)


def dot_nt(a, b):
    return lax.dot_general(a, b, NT, preferred_element_type=F32)


def shifted(x):
    n = x.shape[1]
    lane = lax.broadcasted_iota(jnp.int32, x.shape, 1)
    before = jnp.where(lane == 0, 0.0, pltpu.roll(x, 1, axis=1))
    after = jnp.where(lane == n - 1, 0.0, pltpu.roll(x, n - 1, axis=1))
    return before.astype(BF16), after.astype(BF16)


def exists(gx, gy, sx, sy):
    cond = None
    for ok in (
        [gx < NGX - 1] if sx == 1 else [gx > 0] if sx == -1 else []
    ) + ([gy < NGY - 1] if sy == 1 else [gy > 0] if sy == -1 else []):
        cond = ok if cond is None else jnp.logical_and(cond, ok)
    return cond


def span(s, h, n, sending):
    if s == 0:
        return h, n
    if sending:
        return (n, h) if s == 1 else (h, h)
    return (0, h) if s == 1 else (h + n, h)


class Halo:
    def __init__(self, buf, chan, h, nz, ny, send_sem, recv_sem, gx, gy):
        self.buf, self.chan, self.h, self.nz, self.ny = buf, chan, h, nz, ny
        self.send_sem, self.recv_sem, self.gx, self.gy = send_sem, recv_sem, gx, gy

    def part(self, sx, sy, sending):
        z0, zn = span(sx, self.h, self.nz, sending)
        y0, yn = span(sy, self.h, self.ny, sending)
        return self.buf.at[pl.ds(z0, zn), pl.ds(y0, yn), self.chan, :]

    def desc(self, i):
        sx, sy = DIRS[i]
        return pltpu.make_async_remote_copy(
            src_ref=self.part(sx, sy, True),
            dst_ref=self.part(sx, sy, False),
            send_sem=self.send_sem.at[i],
            recv_sem=self.recv_sem.at[i],
            device_id=(self.gx + sx, self.gy + sy),
            device_id_type=MESH,
        )

    def clear_edges(self):
        h, nz, ny = self.h, self.nz, self.ny
        for s, n, axis, g, last in (
            (-1, nz, 0, self.gx, 0),
            (1, nz, 0, self.gx, NGX - 1),
            (-1, ny, 1, self.gy, 0),
            (1, ny, 1, self.gy, NGY - 1),
        ):
            at = 0 if s == -1 else h + n
            rows = pl.ds(at, h)

            @pl.when(g == last)
            def _(axis=axis, rows=rows):
                index = (rows, slice(None)) if axis == 0 else (slice(None), rows)
                view = self.buf.at[(*index, self.chan, slice(None))]
                view[...] = jnp.zeros(view.shape, view.dtype)

    def start(self):
        for i, (sx, sy) in enumerate(DIRS):

            @pl.when(exists(self.gx, self.gy, sx, sy))
            def _(i=i):
                self.desc(i).start()

    def wait_recv(self):
        for i, (sx, sy) in enumerate(DIRS):

            @pl.when(exists(self.gx, self.gy, -sx, -sy))
            def _(i=i):
                self.desc(i).wait_recv()

    def wait_send(self):
        for i, (sx, sy) in enumerate(DIRS):

            @pl.when(exists(self.gx, self.gy, sx, sy))
            def _(i=i):
                self.desc(i).wait_send()


class AllReduce:
    def __init__(self, terms, rs, bx, fin, sems, na, nb, a, b, dev_a, dev_b):
        self.terms, self.rs, self.bx, self.fin = terms, rs, bx, fin
        self.na, self.nb, self.a, self.b = na, nb, a, b
        self.dev_a, self.dev_b = dev_a, dev_b
        self.rs_s, self.rs_r, self.b_s, self.b_r, self.g_s, self.g_r = sems

    def rs_copy(self, k):
        d = lax.rem(self.a + k, self.na)
        return pltpu.make_async_remote_copy(
            self.terms.at[d], self.rs.at[k], self.rs_s.at[k], self.rs_r.at[k], self.dev_a(d), MESH
        )

    def b_copy(self, k):
        d = lax.rem(self.b + k, self.nb)
        return pltpu.make_async_remote_copy(
            self.bx.at[self.b], self.bx.at[self.b], self.b_s.at[k], self.b_r.at[k], self.dev_b(d), MESH
        )

    def g_copy(self, k):
        d = lax.rem(self.a + k, self.na)
        return pltpu.make_async_remote_copy(
            self.fin.at[self.a], self.fin.at[self.a], self.g_s.at[k], self.g_r.at[k], self.dev_a(d), MESH
        )

    def start_scatter(self):
        for k in range(1, self.na):
            self.rs_copy(k).start()

    def start_exchange(self):
        total = self.terms[self.a]
        for k in range(1, self.na):
            self.rs_copy(k).wait_recv()
        for k in range(1, self.na):
            total = total + self.rs[k]
        self.bx[self.b] = total
        for k in range(1, self.nb):
            self.b_copy(k).start()

    def start_gather(self):
        for k in range(1, self.nb):
            self.b_copy(k).wait_recv()
        total = self.bx[0]
        for k in range(1, self.nb):
            total = total + self.bx[k]
        self.fin[self.a] = total
        for k in range(1, self.na):
            self.g_copy(k).start()

    def finish(self):
        for k in range(1, self.na):
            self.g_copy(k).wait_recv()

    def wait_send(self):
        for k in range(1, self.na):
            self.rs_copy(k).wait_send()
            self.g_copy(k).wait_send()
        for k in range(1, self.nb):
            self.b_copy(k).wait_send()


def kernel(
    vol_hbm, fcot_hbm, ccot_hbm, kf_hbm, kc_hbm,
    fo_ref, co_ref, vg_ref, ffin, cfin,
    raw_v, raw_f, raw_c, kf, kc, st_v, st_f, st_c, st_o, st_co,
    vp, cp, qp, tp, sp, fob, g1, fg, csb, cob, w32, wc32, wft, ft, ct,
    frs, fbx, crs, cbx,
    in_sem, hs, hr, know, f_rs_s, f_rs_r, f_b_s, f_b_r, f_g_s, f_g_r,
    c_rs_s, c_rs_r, c_b_s, c_b_r, c_g_s, c_g_r,
):
    gx, gy = lax.axis_index("gx"), lax.axis_index("gy")
    mid = pl.ds(C1, C1)
    barrier = pltpu.get_barrier_semaphore()
    n_halo = 0
    for sx, sy in DIRS:
        near = exists(gx, gy, sx, sy)
        n_halo = n_halo + near.astype(jnp.int32)

        @pl.when(near)
        def _(sx=sx, sy=sy):
            pl.semaphore_signal(
                barrier, inc=1, device_id=(gx + sx, gy + sy), device_id_type=MESH
            )

    loads = [
        pltpu.make_async_copy(src, dst, in_sem.at[i])
        for i, (src, dst) in enumerate(
            (
                (vol_hbm, raw_v), (kf_hbm, kf), (kc_hbm, kc),
                (ccot_hbm, raw_c), (fcot_hbm, raw_f),
            )
        )
    ]
    for load in loads:
        load.start()

    zi, hi = lax.rem(gx, 4), lax.div(gx, 4)
    y_lo, core = lax.div(gy, 2), lax.rem(gy, 2)
    base = hi * 4

    def c_dev_a(d):
        return (base + lax.div(d, 4), lax.rem(d, 4))

    def c_dev_b(d):
        return (d * 4 + zi, gy)

    def f_dev_a(d):
        return (base + lax.div(d, 2), y_lo * 2 + lax.rem(d, 2))

    def f_dev_b(d):
        return (lax.div(d, 2) * 4 + zi, lax.rem(d, 2) * 2 + core)

    a_c, a_f, b_f = zi * 4 + gy, zi * 2 + core, hi * 2 + y_lo

    def spread_word(step):
        reach = 2 << step
        for side, sign in enumerate((1, -1)):

            @pl.when((gx < NGX - reach) if sign == 1 else (gx >= reach))
            def _(side=side, sign=sign):
                pl.semaphore_signal(
                    know.at[step, side], inc=1,
                    device_id=(gx + sign * reach, gy), device_id_type=MESH,
                )

    def hear_word(step):
        reach = 2 << step
        for side, sign in enumerate((1, -1)):

            @pl.when((gx >= reach) if sign == 1 else (gx < NGX - reach))
            def _(side=side):
                pl.semaphore_wait(know.at[step, side], 1)

    vhalo = Halo(vp, mid, 1, D, R, hs.at[0], hr.at[0], gx, gy)
    chalo = Halo(cp, slice(None), 1, HD, HR, hs.at[1], hr.at[1], gx, gy)
    qhalo = Halo(qp, mid, 2, HD, HR, hs.at[2], hr.at[2], gx, gy)
    shalo = Halo(sp, mid, 1, D, R, hs.at[3], hr.at[3], gx, gy)
    f_sum = AllReduce(
        ft, frs, fbx, ffin, (f_rs_s, f_rs_r, f_b_s, f_b_r, f_g_s, f_g_r),
        8, 16, a_f, b_f, f_dev_a, f_dev_b,
    )
    c_sum = AllReduce(
        ct, crs, cbx, cfin, (c_rs_s, c_rs_r, c_b_s, c_b_r, c_g_s, c_g_r),
        16, 8, a_c, hi, c_dev_a, c_dev_b,
    )
    for halo in (vhalo, chalo, qhalo, shalo):
        halo.clear_edges()

    loads[0].wait()
    for t in range(2):
        st_v[t] = raw_v[:, t * 128 : (t + 1) * 128].astype(F32)
    for z in range(D):
        for y in range(R):
            for t in range(2):
                vp[z + 1, y + 1, mid, pl.ds(t * 128, 128)] = st_v[
                    t, pl.ds(z * R + y, C1, stride=D * R), :
                ].astype(BF16)
    pl.semaphore_wait(barrier, n_halo)
    vhalo.start()

    def put_shifts(buf, z, y, order):
        before, after = shifted(buf[z, y, mid, :].astype(F32))
        low, high = (before, after) if order > 0 else (after, before)
        buf[z, y, pl.ds(0, C1), :] = low
        buf[z, y, pl.ds(2 * C1, C1), :] = high

    def own_shifts(buf, h, nz, ny, order):
        @pl.loop(0, nz)
        def _(z):
            for y in range(ny):
                put_shifts(buf, z + h, y + h, order)

    def halo_shifts(buf, h, nz, ny, order):
        @pl.loop(0, h)
        def _(z):
            for y in range(ny + 2 * h):
                put_shifts(buf, z, y, order)
                put_shifts(buf, z + h + nz, y, order)

        @pl.loop(0, nz)
        def _(z):
            for y in range(h):
                put_shifts(buf, z + h, y, order)
                put_shifts(buf, z + h, y + h + ny, order)

    def taps(buf, z, y, back=False):
        rows = []
        for a in range(3):
            for b in range(3):
                da, db = (2 - a, 2 - b) if back else (a, b)
                rows.append(buf[z + da, y + db])
        return jnp.concatenate(rows, axis=0)

    own_shifts(vp, 1, D, R, 1)
    for one in (1, 2):
        loads[one].wait()
    for tap in range(27):
        w32[:, tap * C1 : (tap + 1) * C1] = kf[tap * C1 : (tap + 1) * C1, :].astype(F32)
        wc32[:, tap * C2 : (tap + 1) * C2] = kc[tap * C1 : (tap + 1) * C1, :].astype(F32)

    def eye(n):
        rows = lax.broadcasted_iota(jnp.int32, (n, n), 0)
        return (rows == lax.broadcasted_iota(jnp.int32, (n, n), 1)).astype(F32).astype(BF16)

    wf = w32[...].astype(BF16)
    wft[...] = dot_nt(eye(C1), kf[...]).astype(BF16)
    loads[3].wait()
    st_c[...] = raw_c[...].astype(F32)
    for z in range(HD):
        for y in range(HR):
            cp[z + 1, y + 1] = st_c[pl.ds(z * HR + y, C2, stride=HD * HR), :].astype(BF16)
    chalo.start()

    def fine_row(z, y):
        pre = dot(wf, taps(vp, z, y))
        s = jax.nn.sigmoid(pre)
        out = (vp[z + 1, y + 1, mid, :].astype(F32) + pre * s).astype(BF16)
        g1[z, y] = s * (1.0 + pre * (1.0 - s))
        fob[z, y] = out

    @pl.loop(1, D - 1)
    def _(z):
        for y in range(1, R - 1):
            fine_row(z, y)

    wc = dot_nt(eye(C2), kc[...]).astype(BF16)
    wct = wc32[...].astype(BF16)
    pool_row = lax.broadcasted_iota(jnp.int32, (W, HW), 0)
    pool_col = lax.broadcasted_iota(jnp.int32, (W, HW), 1)
    pool_mat = (lax.div(pool_row, 2) == pool_col).astype(F32).astype(BF16)
    up_row = lax.broadcasted_iota(jnp.int32, (HW, 3 * W), 0)
    up_col = lax.broadcasted_iota(jnp.int32, (HW, 3 * W), 1)
    up_mat = (
        up_row == lax.div(lax.rem(up_col, W), 2) + 1 - lax.div(up_col, W)
    ).astype(F32).astype(BF16)
    loads[4].wait()
    for t in range(2):
        st_f[t] = raw_f[:, t * 128 : (t + 1) * 128].astype(F32)
    vhalo.wait_recv()
    spread_word(0)
    halo_shifts(vp, 1, D, R, 1)

    @pl.loop(0, 2)
    def _(side):
        for y in range(R):
            fine_row(side * (D - 1), y)
        for y in (0, R - 1):
            fine_row(side + 1, y)

    @pl.loop(0, HD)
    def _(zc):
        for yc in range(HR):
            four = fob[pl.ds(zc * 2, 2), pl.ds(yc * 2, 2)].reshape(4 * C1, W)
            half = dot(four, pool_mat)
            total = half[0:16] + half[16:32] + half[32:48] + half[48:64]
            qp[zc + 2, yc + 2, mid, :] = (total * 0.125).astype(BF16)

    qhalo.start()
    own_shifts(qp, 2, HD, HR, 1)
    hear_word(0)
    spread_word(1)

    def rows_out(rows, store):
        @pl.loop(0, D)
        def _(z):
            for y in range(R):
                value = rows[z, y].astype(F32)
                for t in range(2):
                    store[t, pl.ds(z * R + y, C1, stride=D * R), :] = value[
                        :, t * 128 : (t + 1) * 128
                    ]

    rows_out(fob, st_o)
    for t in range(2):
        fo_ref[:, t * 128 : (t + 1) * 128] = st_o[t].astype(BF16)
    chalo.wait_recv()
    qhalo.wait_recv()
    halo_shifts(qp, 2, HD, HR, 1)

    @pl.loop(0, HD + 2)
    def _(z):
        for y in range(HR + 2):
            pre = dot(wc, taps(qp, z, y))
            s = jax.nn.sigmoid(pre)
            slope = cp[z, y].astype(F32) * (s * (1.0 + pre * (1.0 - s)))
            csb[z, y] = slope.astype(BF16)
            if 1 <= y <= HR:
                cob[z, y - 1] = (pre * s).astype(BF16)
        wide = dot(csb[z].reshape((HR + 2) * C2, HW), up_mat).astype(BF16)
        for c in range(3):
            tp[z, :, pl.ds(c * C2, C2), :] = wide[:, c * W : (c + 1) * W].reshape(HR + 2, C2, W)

    hear_word(1)
    spread_word(2)
    ck = jnp.zeros((C2, 27 * C1), F32)
    for z in range(HD):
        for y in range(HR):
            ck = ck + dot_nt(csb[z + 1, y + 1], taps(qp, z + 1, y + 1))
    ck = jnp.concatenate([ck, jnp.zeros((C2, 80), F32)], axis=1)
    for i in range(4):
        for t in range(4):
            ct[i * 4 + t] = ck[i * 8 : (i + 1) * 8, t * 128 : (t + 1) * 128]
    c_sum.start_scatter()

    @pl.loop(0, HD)
    def _(zc):
        for yc in range(HR):
            spread = dot(wct, taps(tp, zc, yc, True)) * 0.125
            for zz in range(2):
                for yy in range(2):
                    z, y = zc * 2 + zz, yc * 2 + yy
                    cot = jnp.concatenate(
                        [st_f[t, pl.ds(z * R + y, C1, stride=D * R), :] for t in range(2)], axis=1
                    )
                    grad = cot + spread
                    fg[z, y] = grad
                    sp[z + 1, y + 1, mid, :] = (grad * g1[z, y]).astype(BF16)

    shalo.start()
    hear_word(2)
    spread_word(3)

    def fine_terms(z, acc):
        for y in range(R):
            acc = acc + dot_nt(sp[z + 1, y + 1, mid, :], taps(vp, z, y))
        return acc

    fk = lax.fori_loop(0, D, fine_terms, jnp.zeros((C1, 27 * C1), F32))
    fk = jnp.concatenate([fk, jnp.zeros((C1, 80), F32)], axis=1)
    for i in range(2):
        for t in range(4):
            ft[i * 4 + t] = fk[i * 8 : (i + 1) * 8, t * 128 : (t + 1) * 128]
    f_sum.start_scatter()
    hear_word(3)
    c_sum.start_exchange()
    own_shifts(sp, 1, D, R, -1)
    f_sum.start_exchange()
    shalo.wait_recv()
    halo_shifts(sp, 1, D, R, -1)
    wft_v = wft[...]

    @pl.loop(0, D)
    def _(z):
        for y in range(R):
            fg[z, y] = fg[z, y] + dot(wft_v, taps(sp, z, y, True))

    c_sum.start_gather()
    f_sum.start_gather()
    rows_out(fg, st_o)
    for t in range(2):
        vg_ref[:, t * 128 : (t + 1) * 128] = st_o[t].astype(BF16)
    for z in range(HD):
        for y in range(HR):
            st_co[pl.ds(z * HR + y, C2, stride=HD * HR), :] = cob[z + 1, y].astype(F32)
    co_ref[...] = st_co[...].astype(BF16)
    for one in (vhalo, chalo, qhalo, shalo):
        one.wait_send()
    c_sum.finish()
    f_sum.finish()
    for one in (c_sum, f_sum):
        one.wait_send()


def emit_kernel(fo, co, vg, ffin, cfin, fo_hbm, co_hbm, vg_hbm, fk_hbm, ck_hbm, fk, ck, sem):
    copies = [
        pltpu.make_async_copy(src, dst, sem.at[i])
        for i, (src, dst) in enumerate(
            ((fo, fo_hbm), (vg, vg_hbm), (co, co_hbm), (fk, fk_hbm), (ck, ck_hbm))
        )
    ]
    for i in range(3):
        copies[i].start()
    for i in range(2):
        for t in range(4):
            tile = ffin[i * 4 + t] * (1048576.0**-0.5)
            for k in range(8):
                tap = t * 8 + k
                if tap < 27:
                    fk[tap, pl.ds(i * 8, 8), :] = tile[:, k * C1 : (k + 1) * C1]
    copies[3].start()
    for t in range(4):
        rows = jnp.concatenate([cfin[i * 4 + t] for i in range(4)], axis=0)
        cols = jnp.transpose(rows * (131072.0**-0.5))
        for k in range(8):
            tap = t * 8 + k
            if tap < 27:
                ck[tap] = cols[k * C1 : (k + 1) * C1, :]
    copies[4].start()
    for one in copies:
        one.wait()


def local(volume, fine_kernel, coarse_kernel, fine_cotangent, coarse_cotangent):
    kf = fine_kernel.reshape(27 * C1, C1)
    kc = coarse_kernel.transpose(0, 1, 2, 4, 3).reshape(27 * C1, C2)
    hbm = pl.BlockSpec(memory_space=pltpu.HBM)
    vmem = pl.BlockSpec(memory_space=pltpu.VMEM)
    dma = pltpu.SemaphoreType.DMA
    V = pltpu.VMEM
    tile = (8, 128)
    fine, coarse = (C1 * D * R, W), (C2 * HD * HR, HW)
    parts = pl.pallas_call(
        kernel,
        out_shape=[
            jax.ShapeDtypeStruct(fine, BF16),
            jax.ShapeDtypeStruct(coarse, BF16),
            jax.ShapeDtypeStruct(fine, BF16),
            jax.ShapeDtypeStruct((8, *tile), F32),
            jax.ShapeDtypeStruct((16, *tile), F32),
        ],
        in_specs=[hbm] * 5,
        out_specs=[vmem] * 5,
        scratch_shapes=[
            V(fine, BF16), V(fine, BF16), V(coarse, BF16),
            V((27 * C1, C1), BF16), V((27 * C1, C2), BF16),
            V((2, C1 * D * R, 128), F32), V((2, C1 * D * R, 128), F32), V(coarse, F32),
            V((2, C1 * D * R, 128), F32), V(coarse, F32),
            V((D + 2, R + 2, 3 * C1, W), BF16),
            V((HD + 2, HR + 2, C2, HW), BF16),
            V((HD + 4, HR + 4, 3 * C1, HW), BF16),
            V((HD + 2, HR + 2, 3 * C2, W), BF16),
            V((D + 2, R + 2, 3 * C1, W), BF16),
            V((D, R, C1, W), BF16), V((D, R, C1, W), F32), V((D, R, C1, W), F32),
            V((HD + 2, HR + 2, C2, HW), BF16), V((HD + 2, HR, C2, HW), BF16),
            V((C1, 27 * C1), F32), V((C1, 27 * C2), F32), V((C1, 27 * C1), BF16),
            V((8, *tile), F32), V((16, *tile), F32),
            V((8, *tile), F32), V((16, *tile), F32),
            V((16, *tile), F32), V((8, *tile), F32),
            dma((5,)), dma((4, 8)), dma((4, 8)), pltpu.SemaphoreType.REGULAR((4, 2)),
            dma((8,)), dma((8,)), dma((16,)), dma((16,)), dma((8,)), dma((8,)),
            dma((16,)), dma((16,)), dma((8,)), dma((8,)), dma((16,)), dma((16,)),
        ],
        compiler_params=pltpu.CompilerParams(
            collective_id=0, has_side_effects=True, vmem_limit_bytes=48 << 20
        ),
        name="unet_levels",
    )(
        *(
            pltpu.with_memory_space_constraint(value, pltpu.HBM)
            for value in (
                volume.reshape(fine), fine_cotangent.reshape(fine),
                coarse_cotangent.reshape(coarse), kf, kc,
            )
        )
    )
    fo, co, vg, fk, ck = pl.pallas_call(
        emit_kernel,
        out_shape=[
            jax.ShapeDtypeStruct(fine, BF16),
            jax.ShapeDtypeStruct(coarse, BF16),
            jax.ShapeDtypeStruct(fine, BF16),
            jax.ShapeDtypeStruct((27, C1, C1), F32),
            jax.ShapeDtypeStruct((27, C1, C2), F32),
        ],
        in_specs=[vmem] * 5,
        out_specs=[hbm] * 5,
        scratch_shapes=[V((27, C1, C1), F32), V((27, C1, C2), F32), dma((5,))],
        compiler_params=pltpu.CompilerParams(vmem_limit_bytes=8 << 20),
        name="emit",
    )(*parts)
    return (
        fo.reshape(volume.shape),
        co.reshape(coarse_cotangent.shape),
        vg.reshape(volume.shape),
        fk.reshape(fine_kernel.shape),
        ck.reshape(3, 3, 3, C1, C2).transpose(0, 1, 2, 4, 3),
    )


def solution(mesh):
    block = P(None, "gx", "gy", None)
    return jax.shard_map(
        local,
        mesh=mesh,
        in_specs=(block, P(), P(), block, block),
        out_specs=(block, block, block, P(), P()),
        check_vma=False,
    )
```

```python
import jax
import jax.numpy as jnp
from jax import lax
from jax.experimental import pallas as pl
from jax.experimental.pallas import tpu as pltpu
from jax.sharding import PartitionSpec as P

F32 = jnp.float32
BF16 = jnp.bfloat16
MESH = pl.DeviceIdType.MESH
C1, C2 = 16, 32
D, R, W = 4, 8, 256
HD, HR, HW = 2, 4, 128
NGX, NGY = 32, 4
DIRS = [(sx, sy) for sx in (-1, 0, 1) for sy in (-1, 0, 1) if (sx, sy) != (0, 0)]
NT = (((1,), (1,)), ((), ()))


def dot(a, b):
    return jnp.dot(a, b, preferred_element_type=F32)


def dot_nt(a, b):
    return lax.dot_general(a, b, NT, preferred_element_type=F32)


def shifted(x):
    n = x.shape[1]
    lane = lax.broadcasted_iota(jnp.int32, x.shape, 1)
    before = jnp.where(lane == 0, 0.0, pltpu.roll(x, 1, axis=1))
    after = jnp.where(lane == n - 1, 0.0, pltpu.roll(x, n - 1, axis=1))
    return before.astype(BF16), after.astype(BF16)


def exists(gx, gy, sx, sy):
    cond = None
    for ok in (
        [gx < NGX - 1] if sx == 1 else [gx > 0] if sx == -1 else []
    ) + ([gy < NGY - 1] if sy == 1 else [gy > 0] if sy == -1 else []):
        cond = ok if cond is None else jnp.logical_and(cond, ok)
    return cond


def span(s, h, n, sending):
    if s == 0:
        return h, n
    if sending:
        return (n, h) if s == 1 else (h, h)
    return (0, h) if s == 1 else (h + n, h)


class Halo:
    def __init__(self, buf, chan, h, nz, ny, send_sem, recv_sem, gx, gy):
        self.buf, self.chan, self.h, self.nz, self.ny = buf, chan, h, nz, ny
        self.send_sem, self.recv_sem, self.gx, self.gy = send_sem, recv_sem, gx, gy

    def part(self, sx, sy, sending):
        z0, zn = span(sx, self.h, self.nz, sending)
        y0, yn = span(sy, self.h, self.ny, sending)
        return self.buf.at[pl.ds(z0, zn), pl.ds(y0, yn), self.chan, :]

    def desc(self, i):
        sx, sy = DIRS[i]
        return pltpu.make_async_remote_copy(
            src_ref=self.part(sx, sy, True),
            dst_ref=self.part(sx, sy, False),
            send_sem=self.send_sem.at[i],
            recv_sem=self.recv_sem.at[i],
            device_id=(self.gx + sx, self.gy + sy),
            device_id_type=MESH,
        )

    def clear_edges(self):
        h, nz, ny = self.h, self.nz, self.ny
        for s, n, axis, g, last in (
            (-1, nz, 0, self.gx, 0),
            (1, nz, 0, self.gx, NGX - 1),
            (-1, ny, 1, self.gy, 0),
            (1, ny, 1, self.gy, NGY - 1),
        ):
            at = 0 if s == -1 else h + n
            rows = pl.ds(at, h)

            @pl.when(g == last)
            def _(axis=axis, rows=rows):
                index = (rows, slice(None)) if axis == 0 else (slice(None), rows)
                view = self.buf.at[(*index, self.chan, slice(None))]
                view[...] = jnp.zeros(view.shape, view.dtype)

    def start(self):
        for i, (sx, sy) in enumerate(DIRS):

            @pl.when(exists(self.gx, self.gy, sx, sy))
            def _(i=i):
                self.desc(i).start()

    def wait_recv(self):
        for i, (sx, sy) in enumerate(DIRS):

            @pl.when(exists(self.gx, self.gy, -sx, -sy))
            def _(i=i):
                self.desc(i).wait_recv()

    def wait_send(self):
        for i, (sx, sy) in enumerate(DIRS):

            @pl.when(exists(self.gx, self.gy, sx, sy))
            def _(i=i):
                self.desc(i).wait_send()


class AllReduce:
    def __init__(self, terms, rs, bx, fin, sems, na, nb, a, b, dev_a, dev_b):
        self.terms, self.rs, self.bx, self.fin = terms, rs, bx, fin
        self.na, self.nb, self.a, self.b = na, nb, a, b
        self.dev_a, self.dev_b = dev_a, dev_b
        self.rs_s, self.rs_r, self.b_s, self.b_r, self.g_s, self.g_r = sems

    def rs_copy(self, k):
        d = lax.rem(self.a + k, self.na)
        return pltpu.make_async_remote_copy(
            self.terms.at[d], self.rs.at[k], self.rs_s.at[k], self.rs_r.at[k], self.dev_a(d), MESH
        )

    def b_copy(self, k):
        d = lax.rem(self.b + k, self.nb)
        return pltpu.make_async_remote_copy(
            self.bx.at[self.b], self.bx.at[self.b], self.b_s.at[k], self.b_r.at[k], self.dev_b(d), MESH
        )

    def g_copy(self, k):
        d = lax.rem(self.a + k, self.na)
        return pltpu.make_async_remote_copy(
            self.fin.at[self.a], self.fin.at[self.a], self.g_s.at[k], self.g_r.at[k], self.dev_a(d), MESH
        )

    def start_scatter(self):
        for k in range(1, self.na):
            self.rs_copy(k).start()

    def start_exchange(self):
        total = self.terms[self.a]
        for k in range(1, self.na):
            self.rs_copy(k).wait_recv()
        for k in range(1, self.na):
            total = total + self.rs[k]
        self.bx[self.b] = total
        for k in range(1, self.nb):
            self.b_copy(k).start()

    def start_gather(self):
        for k in range(1, self.nb):
            self.b_copy(k).wait_recv()
        total = self.bx[0]
        for k in range(1, self.nb):
            total = total + self.bx[k]
        self.fin[self.a] = total
        for k in range(1, self.na):
            self.g_copy(k).start()

    def finish(self):
        for k in range(1, self.na):
            self.g_copy(k).wait_recv()

    def wait_send(self):
        for k in range(1, self.na):
            self.rs_copy(k).wait_send()
            self.g_copy(k).wait_send()
        for k in range(1, self.nb):
            self.b_copy(k).wait_send()


def kernel(
    vol_hbm, fcot_hbm, ccot_hbm, kf_hbm, kc_hbm,
    fo_ref, co_ref, vg_ref, ffin, cfin,
    raw_v, raw_f, raw_c, kf, kc, st_v, st_f, st_c, st_o, st_co,
    vp, cp, qp, tp, sp, fob, g1, fg, csb, cob, w32, wc32, wft, terms, ft, ct,
    frs, fbx, crs, cbx,
    in_sem, hs, hr, know, f_rs_s, f_rs_r, f_b_s, f_b_r, f_g_s, f_g_r,
    c_rs_s, c_rs_r, c_b_s, c_b_r, c_g_s, c_g_r,
):
    gx, gy = lax.axis_index("gx"), lax.axis_index("gy")
    mid = pl.ds(C1, C1)
    barrier = pltpu.get_barrier_semaphore()
    n_halo = 0
    for sx, sy in DIRS:
        near = exists(gx, gy, sx, sy)
        n_halo = n_halo + near.astype(jnp.int32)

        @pl.when(near)
        def _(sx=sx, sy=sy):
            pl.semaphore_signal(
                barrier, inc=1, device_id=(gx + sx, gy + sy), device_id_type=MESH
            )

    loads = [
        pltpu.make_async_copy(src, dst, in_sem.at[i])
        for i, (src, dst) in enumerate(
            (
                (vol_hbm, raw_v), (kf_hbm, kf), (kc_hbm, kc),
                (ccot_hbm, raw_c), (fcot_hbm, raw_f),
            )
        )
    ]
    for load in loads:
        load.start()

    zi, hi = lax.rem(gx, 4), lax.div(gx, 4)
    y_lo, core = lax.div(gy, 2), lax.rem(gy, 2)
    base = hi * 4

    def c_dev_a(d):
        return (base + lax.div(d, 4), lax.rem(d, 4))

    def c_dev_b(d):
        return (d * 4 + zi, gy)

    def f_dev_a(d):
        return (base + lax.div(d, 2), y_lo * 2 + lax.rem(d, 2))

    def f_dev_b(d):
        return (lax.div(d, 2) * 4 + zi, lax.rem(d, 2) * 2 + core)

    a_c, a_f, b_f = zi * 4 + gy, zi * 2 + core, hi * 2 + y_lo

    def spread_word(step):
        reach = 2 << step
        for side, sign in enumerate((1, -1)):

            @pl.when((gx < NGX - reach) if sign == 1 else (gx >= reach))
            def _(side=side, sign=sign):
                pl.semaphore_signal(
                    know.at[step, side], inc=1,
                    device_id=(gx + sign * reach, gy), device_id_type=MESH,
                )

    def hear_word(step):
        reach = 2 << step
        for side, sign in enumerate((1, -1)):

            @pl.when((gx >= reach) if sign == 1 else (gx < NGX - reach))
            def _(side=side):
                pl.semaphore_wait(know.at[step, side], 1)

    vhalo = Halo(vp, mid, 1, D, R, hs.at[0], hr.at[0], gx, gy)
    chalo = Halo(cp, slice(None), 1, HD, HR, hs.at[1], hr.at[1], gx, gy)
    qhalo = Halo(qp, mid, 2, HD, HR, hs.at[2], hr.at[2], gx, gy)
    shalo = Halo(sp, mid, 1, D, R, hs.at[3], hr.at[3], gx, gy)
    f_sum = AllReduce(
        ft, frs, fbx, ffin, (f_rs_s, f_rs_r, f_b_s, f_b_r, f_g_s, f_g_r),
        8, 16, a_f, b_f, f_dev_a, f_dev_b,
    )
    c_sum = AllReduce(
        ct, crs, cbx, cfin, (c_rs_s, c_rs_r, c_b_s, c_b_r, c_g_s, c_g_r),
        16, 8, a_c, hi, c_dev_a, c_dev_b,
    )
    for halo in (vhalo, chalo, qhalo, shalo):
        halo.clear_edges()

    loads[0].wait()
    for t in range(2):
        st_v[t] = raw_v[:, t * 128 : (t + 1) * 128].astype(F32)
    for z in range(D):
        for y in range(R):
            for t in range(2):
                vp[z + 1, y + 1, mid, pl.ds(t * 128, 128)] = st_v[
                    t, pl.ds(z * R + y, C1, stride=D * R), :
                ].astype(BF16)
    pl.semaphore_wait(barrier, n_halo)
    vhalo.start()

    def put_shifts(buf, z, y, order):
        before, after = shifted(buf[z, y, mid, :].astype(F32))
        low, high = (before, after) if order > 0 else (after, before)
        buf[z, y, pl.ds(0, C1), :] = low
        buf[z, y, pl.ds(2 * C1, C1), :] = high

    def own_shifts(buf, h, nz, ny, order):
        @pl.loop(0, nz)
        def _(z):
            for y in range(ny):
                put_shifts(buf, z + h, y + h, order)

    def halo_shifts(buf, h, nz, ny, order):
        @pl.loop(0, h)
        def _(z):
            for y in range(ny + 2 * h):
                put_shifts(buf, z, y, order)
                put_shifts(buf, z + h + nz, y, order)

        @pl.loop(0, nz)
        def _(z):
            for y in range(h):
                put_shifts(buf, z + h, y, order)
                put_shifts(buf, z + h, y + h + ny, order)

    def taps(buf, z, y, back=False):
        rows = []
        for a in range(3):
            for b in range(3):
                da, db = (2 - a, 2 - b) if back else (a, b)
                rows.append(buf[z + da, y + db])
        return jnp.concatenate(rows, axis=0)

    own_shifts(vp, 1, D, R, 1)
    for one in (1, 2):
        loads[one].wait()
    for tap in range(27):
        w32[:, tap * C1 : (tap + 1) * C1] = kf[tap * C1 : (tap + 1) * C1, :].astype(F32)
        wc32[:, tap * C2 : (tap + 1) * C2] = kc[tap * C1 : (tap + 1) * C1, :].astype(F32)

    def eye(n):
        rows = lax.broadcasted_iota(jnp.int32, (n, n), 0)
        return (rows == lax.broadcasted_iota(jnp.int32, (n, n), 1)).astype(F32).astype(BF16)

    wf = w32[...].astype(BF16)
    wft[...] = dot_nt(eye(C1), kf[...]).astype(BF16)
    loads[3].wait()
    st_c[...] = raw_c[...].astype(F32)
    for z in range(HD):
        for y in range(HR):
            cp[z + 1, y + 1] = st_c[pl.ds(z * HR + y, C2, stride=HD * HR), :].astype(BF16)
    chalo.start()

    def fine_row(z, y):
        pre = dot(wf, taps(vp, z, y))
        s = jax.nn.sigmoid(pre)
        out = (vp[z + 1, y + 1, mid, :].astype(F32) + pre * s).astype(BF16)
        g1[z, y] = s * (1.0 + pre * (1.0 - s))
        fob[z, y] = out

    @pl.loop(1, D - 1)
    def _(z):
        for y in range(1, R - 1):
            fine_row(z, y)

    wc = dot_nt(eye(C2), kc[...]).astype(BF16)
    wct = wc32[...].astype(BF16)
    pool_row = lax.broadcasted_iota(jnp.int32, (W, HW), 0)
    pool_col = lax.broadcasted_iota(jnp.int32, (W, HW), 1)
    pool_mat = (lax.div(pool_row, 2) == pool_col).astype(F32).astype(BF16)
    up_row = lax.broadcasted_iota(jnp.int32, (HW, 3 * W), 0)
    up_col = lax.broadcasted_iota(jnp.int32, (HW, 3 * W), 1)
    up_mat = (
        up_row == lax.div(lax.rem(up_col, W), 2) + 1 - lax.div(up_col, W)
    ).astype(F32).astype(BF16)
    loads[4].wait()
    for t in range(2):
        st_f[t] = raw_f[:, t * 128 : (t + 1) * 128].astype(F32)
    vhalo.wait_recv()
    spread_word(0)
    halo_shifts(vp, 1, D, R, 1)

    @pl.loop(0, 2)
    def _(side):
        for y in range(R):
            fine_row(side * (D - 1), y)
        for y in (0, R - 1):
            fine_row(side + 1, y)

    @pl.loop(0, HD)
    def _(zc):
        for yc in range(HR):
            four = fob[pl.ds(zc * 2, 2), pl.ds(yc * 2, 2)].reshape(4 * C1, W)
            half = dot(four, pool_mat)
            total = half[0:16] + half[16:32] + half[32:48] + half[48:64]
            qp[zc + 2, yc + 2, mid, :] = (total * 0.125).astype(BF16)

    qhalo.start()
    own_shifts(qp, 2, HD, HR, 1)
    hear_word(0)
    spread_word(1)

    def rows_out(rows, store):
        @pl.loop(0, D)
        def _(z):
            for y in range(R):
                value = rows[z, y].astype(F32)
                for t in range(2):
                    store[t, pl.ds(z * R + y, C1, stride=D * R), :] = value[
                        :, t * 128 : (t + 1) * 128
                    ]

    rows_out(fob, st_o)
    for t in range(2):
        fo_ref[:, t * 128 : (t + 1) * 128] = st_o[t].astype(BF16)
    chalo.wait_recv()
    qhalo.wait_recv()
    hear_word(1)
    spread_word(2)
    halo_shifts(qp, 2, HD, HR, 1)

    @pl.loop(0, HD + 2)
    def _(z):
        for y0 in range(0, HR + 2, 2):
            pair = dot(wc, jnp.concatenate([taps(qp, z, y0), taps(qp, z, y0 + 1)], axis=1))
            for y in (y0, y0 + 1):
                pre = pair[:, (y - y0) * HW : (y - y0 + 1) * HW]
                s = jax.nn.sigmoid(pre)
                slope = cp[z, y].astype(F32) * (s * (1.0 + pre * (1.0 - s)))
                csb[z, y] = slope.astype(BF16)
                if 1 <= y <= HR:
                    cob[z, y - 1] = (pre * s).astype(BF16)
        wide = dot(csb[z].reshape((HR + 2) * C2, HW), up_mat).astype(BF16)
        for c in range(3):
            tp[z, :, pl.ds(c * C2, C2), :] = wide[:, c * W : (c + 1) * W].reshape(HR + 2, C2, W)

    def across(rows):
        rows = jnp.concatenate([rows, jnp.zeros((80, rows.shape[1]), F32)], axis=0)
        return jnp.transpose(rows)

    cells = [(z + 1, y + 1) for z in range(HD) for y in range(HR)]
    ck = dot_nt(
        jnp.concatenate([taps(qp, *at) for at in cells], axis=1),
        jnp.concatenate([csb[at] for at in cells], axis=1),
    )
    ck = across(ck)
    for i in range(4):
        for t in range(4):
            ct[i * 4 + t] = ck[i * 8 : (i + 1) * 8, t * 128 : (t + 1) * 128]
    c_sum.start_scatter()

    @pl.loop(0, HD)
    def _(zc):
        for yc in range(HR):
            spread = dot(wct, taps(tp, zc, yc, True)) * 0.125
            for zz in range(2):
                for yy in range(2):
                    z, y = zc * 2 + zz, yc * 2 + yy
                    cot = jnp.concatenate(
                        [st_f[t, pl.ds(z * R + y, C1, stride=D * R), :] for t in range(2)], axis=1
                    )
                    grad = cot + spread
                    fg[z, y] = grad
                    sp[z + 1, y + 1, mid, :] = (grad * g1[z, y]).astype(BF16)

    shalo.start()
    hear_word(2)
    spread_word(3)

    terms[...] = jnp.zeros(terms.shape, F32)

    @pl.loop(0, D)
    def _(z):
        slopes = jnp.concatenate([sp[z + 1, y + 1, mid, :] for y in range(R)], axis=1)
        terms[...] += dot_nt(
            jnp.concatenate([taps(vp, z, y) for y in range(R)], axis=1), slopes
        )

    fk = across(terms[...])
    for i in range(2):
        for t in range(4):
            ft[i * 4 + t] = fk[i * 8 : (i + 1) * 8, t * 128 : (t + 1) * 128]
    f_sum.start_scatter()
    hear_word(3)
    c_sum.start_exchange()
    own_shifts(sp, 1, D, R, -1)
    f_sum.start_exchange()
    shalo.wait_recv()
    halo_shifts(sp, 1, D, R, -1)
    wft_v = wft[...]

    @pl.loop(0, D)
    def _(z):
        for y in range(R):
            fg[z, y] = fg[z, y] + dot(wft_v, taps(sp, z, y, True))

    c_sum.start_gather()
    f_sum.start_gather()
    rows_out(fg, st_o)
    for t in range(2):
        vg_ref[:, t * 128 : (t + 1) * 128] = st_o[t].astype(BF16)
    for z in range(HD):
        for y in range(HR):
            st_co[pl.ds(z * HR + y, C2, stride=HD * HR), :] = cob[z + 1, y].astype(F32)
    co_ref[...] = st_co[...].astype(BF16)
    for one in (vhalo, chalo, qhalo, shalo, c_sum, f_sum):
        one.wait_send()
    c_sum.finish()
    f_sum.finish()


def emit_kernel(fo, co, vg, ffin, cfin, fo_hbm, co_hbm, vg_hbm, fk_hbm, ck_hbm, fk, ck, sem):
    copies = [
        pltpu.make_async_copy(src, dst, sem.at[i])
        for i, (src, dst) in enumerate(
            ((fo, fo_hbm), (vg, vg_hbm), (co, co_hbm), (fk, fk_hbm), (ck, ck_hbm))
        )
    ]
    for i in range(3):
        copies[i].start()
    for i in range(2):
        for t in range(4):
            tile = ffin[i * 4 + t] * (1048576.0**-0.5)
            for k in range(8):
                tap = t * 8 + k
                if tap < 27:
                    fk[tap, pl.ds(i * 8, 8), :] = tile[:, k * C1 : (k + 1) * C1]
    copies[3].start()
    for t in range(4):
        rows = jnp.concatenate([cfin[i * 4 + t] for i in range(4)], axis=0)
        cols = jnp.transpose(rows * (131072.0**-0.5))
        for k in range(8):
            tap = t * 8 + k
            if tap < 27:
                ck[tap] = cols[k * C1 : (k + 1) * C1, :]
    copies[4].start()
    for one in copies:
        one.wait()


def local(volume, fine_kernel, coarse_kernel, fine_cotangent, coarse_cotangent):
    kf = fine_kernel.reshape(27 * C1, C1)
    kc = coarse_kernel.transpose(0, 1, 2, 4, 3).reshape(27 * C1, C2)
    hbm = pl.BlockSpec(memory_space=pltpu.HBM)
    vmem = pl.BlockSpec(memory_space=pltpu.VMEM)
    dma = pltpu.SemaphoreType.DMA
    V = pltpu.VMEM
    tile = (8, 128)
    fine, coarse = (C1 * D * R, W), (C2 * HD * HR, HW)
    parts = pl.pallas_call(
        kernel,
        out_shape=[
            jax.ShapeDtypeStruct(fine, BF16),
            jax.ShapeDtypeStruct(coarse, BF16),
            jax.ShapeDtypeStruct(fine, BF16),
            jax.ShapeDtypeStruct((8, *tile), F32),
            jax.ShapeDtypeStruct((16, *tile), F32),
        ],
        in_specs=[hbm] * 5,
        out_specs=[vmem] * 5,
        scratch_shapes=[
            V(fine, BF16), V(fine, BF16), V(coarse, BF16),
            V((27 * C1, C1), BF16), V((27 * C1, C2), BF16),
            V((2, C1 * D * R, 128), F32), V((2, C1 * D * R, 128), F32), V(coarse, F32),
            V((2, C1 * D * R, 128), F32), V(coarse, F32),
            V((D + 2, R + 2, 3 * C1, W), BF16),
            V((HD + 2, HR + 2, C2, HW), BF16),
            V((HD + 4, HR + 4, 3 * C1, HW), BF16),
            V((HD + 2, HR + 2, 3 * C2, W), BF16),
            V((D + 2, R + 2, 3 * C1, W), BF16),
            V((D, R, C1, W), BF16), V((D, R, C1, W), F32), V((D, R, C1, W), F32),
            V((HD + 2, HR + 2, C2, HW), BF16), V((HD + 2, HR, C2, HW), BF16),
            V((C1, 27 * C1), F32), V((C1, 27 * C2), F32), V((C1, 27 * C1), BF16), V((27 * C1, C1), F32),
            V((8, *tile), F32), V((16, *tile), F32),
            V((8, *tile), F32), V((16, *tile), F32),
            V((16, *tile), F32), V((8, *tile), F32),
            dma((5,)), dma((4, 8)), dma((4, 8)), pltpu.SemaphoreType.REGULAR((4, 2)),
            dma((8,)), dma((8,)), dma((16,)), dma((16,)), dma((8,)), dma((8,)),
            dma((16,)), dma((16,)), dma((8,)), dma((8,)), dma((16,)), dma((16,)),
        ],
        compiler_params=pltpu.CompilerParams(
            collective_id=0, has_side_effects=True, vmem_limit_bytes=48 << 20
        ),
        name="unet_levels",
    )(
        *(
            pltpu.with_memory_space_constraint(value, pltpu.HBM)
            for value in (
                volume.reshape(fine), fine_cotangent.reshape(fine),
                coarse_cotangent.reshape(coarse), kf, kc,
            )
        )
    )
    fo, co, vg, fk, ck = pl.pallas_call(
        emit_kernel,
        out_shape=[
            jax.ShapeDtypeStruct(fine, BF16),
            jax.ShapeDtypeStruct(coarse, BF16),
            jax.ShapeDtypeStruct(fine, BF16),
            jax.ShapeDtypeStruct((27, C1, C1), F32),
            jax.ShapeDtypeStruct((27, C1, C2), F32),
        ],
        in_specs=[vmem] * 5,
        out_specs=[hbm] * 5,
        scratch_shapes=[V((27, C1, C1), F32), V((27, C1, C2), F32), dma((5,))],
        compiler_params=pltpu.CompilerParams(vmem_limit_bytes=8 << 20),
        name="emit",
    )(*parts)
    return (
        fo.reshape(volume.shape),
        co.reshape(coarse_cotangent.shape),
        vg.reshape(volume.shape),
        fk.reshape(fine_kernel.shape),
        ck.reshape(3, 3, 3, C1, C2).transpose(0, 1, 2, 4, 3),
    )


def solution(mesh):
    block = P(None, "gx", "gy", None)
    return jax.shard_map(
        local,
        mesh=mesh,
        in_specs=(block, P(), P(), block, block),
        out_specs=(block, block, block, P(), P()),
        check_vma=False,
    )
```

```python
import jax
import jax.numpy as jnp
from jax import lax
from jax.experimental import pallas as pl
from jax.experimental.pallas import tpu as pltpu
from jax.sharding import PartitionSpec as P

F32 = jnp.float32
BF16 = jnp.bfloat16
MESH = pl.DeviceIdType.MESH
C1, C2 = 16, 32
D, R, W = 4, 8, 256
HD, HR, HW = 2, 4, 128
NGX, NGY = 32, 4
DIRS = [(sx, sy) for sx in (-1, 0, 1) for sy in (-1, 0, 1) if (sx, sy) != (0, 0)]
NT = (((1,), (1,)), ((), ()))


def dot(a, b):
    return jnp.dot(a, b, preferred_element_type=F32)


def dot_nt(a, b):
    return lax.dot_general(a, b, NT, preferred_element_type=F32)


def shifted(x):
    n = x.shape[1]
    lane = lax.broadcasted_iota(jnp.int32, x.shape, 1)
    before = jnp.where(lane == 0, 0.0, pltpu.roll(x, 1, axis=1))
    after = jnp.where(lane == n - 1, 0.0, pltpu.roll(x, n - 1, axis=1))
    return before.astype(BF16), after.astype(BF16)


def exists(gx, gy, sx, sy):
    cond = None
    for ok in (
        [gx < NGX - 1] if sx == 1 else [gx > 0] if sx == -1 else []
    ) + ([gy < NGY - 1] if sy == 1 else [gy > 0] if sy == -1 else []):
        cond = ok if cond is None else jnp.logical_and(cond, ok)
    return cond


def span(s, h, n, sending):
    if s == 0:
        return h, n
    if sending:
        return (n, h) if s == 1 else (h, h)
    return (0, h) if s == 1 else (h + n, h)


class Halo:
    def __init__(self, buf, chan, h, nz, ny, send_sem, recv_sem, gx, gy):
        self.buf, self.chan, self.h, self.nz, self.ny = buf, chan, h, nz, ny
        self.send_sem, self.recv_sem, self.gx, self.gy = send_sem, recv_sem, gx, gy

    def part(self, sx, sy, sending):
        z0, zn = span(sx, self.h, self.nz, sending)
        y0, yn = span(sy, self.h, self.ny, sending)
        return self.buf.at[pl.ds(z0, zn), pl.ds(y0, yn), self.chan, :]

    def desc(self, i):
        sx, sy = DIRS[i]
        return pltpu.make_async_remote_copy(
            src_ref=self.part(sx, sy, True),
            dst_ref=self.part(sx, sy, False),
            send_sem=self.send_sem.at[i],
            recv_sem=self.recv_sem.at[i],
            device_id=(self.gx + sx, self.gy + sy),
            device_id_type=MESH,
        )

    def clear_edges(self):
        h, nz, ny = self.h, self.nz, self.ny
        for s, n, axis, g, last in (
            (-1, nz, 0, self.gx, 0),
            (1, nz, 0, self.gx, NGX - 1),
            (-1, ny, 1, self.gy, 0),
            (1, ny, 1, self.gy, NGY - 1),
        ):
            at = 0 if s == -1 else h + n
            rows = pl.ds(at, h)

            @pl.when(g == last)
            def _(axis=axis, rows=rows):
                index = (rows, slice(None)) if axis == 0 else (slice(None), rows)
                view = self.buf.at[(*index, self.chan, slice(None))]
                view[...] = jnp.zeros(view.shape, view.dtype)

    def start(self):
        for i, (sx, sy) in enumerate(DIRS):

            @pl.when(exists(self.gx, self.gy, sx, sy))
            def _(i=i):
                self.desc(i).start()

    def wait_recv(self):
        for i, (sx, sy) in enumerate(DIRS):

            @pl.when(exists(self.gx, self.gy, -sx, -sy))
            def _(i=i):
                self.desc(i).wait_recv()

    def wait_send(self):
        for i, (sx, sy) in enumerate(DIRS):

            @pl.when(exists(self.gx, self.gy, sx, sy))
            def _(i=i):
                self.desc(i).wait_send()


class AllReduce:
    def __init__(self, terms, rs, bx, fin, sems, na, nb, a, b, dev_a, dev_b):
        self.terms, self.rs, self.bx, self.fin = terms, rs, bx, fin
        self.na, self.nb, self.a, self.b = na, nb, a, b
        self.dev_a, self.dev_b = dev_a, dev_b
        self.rs_s, self.rs_r, self.b_s, self.b_r, self.g_s, self.g_r = sems

    def rs_copy(self, k):
        d = lax.rem(self.a + k, self.na)
        return pltpu.make_async_remote_copy(
            self.terms.at[d], self.rs.at[k], self.rs_s.at[k], self.rs_r.at[k], self.dev_a(d), MESH
        )

    def b_copy(self, k):
        d = lax.rem(self.b + k, self.nb)
        return pltpu.make_async_remote_copy(
            self.bx.at[self.b], self.bx.at[self.b], self.b_s.at[k], self.b_r.at[k], self.dev_b(d), MESH
        )

    def g_copy(self, k):
        d = lax.rem(self.a + k, self.na)
        return pltpu.make_async_remote_copy(
            self.fin.at[self.a], self.fin.at[self.a], self.g_s.at[k], self.g_r.at[k], self.dev_a(d), MESH
        )

    def start_scatter(self):
        for k in range(1, self.na):
            self.rs_copy(k).start()

    def start_exchange(self):
        total = self.terms[self.a]
        for k in range(1, self.na):
            self.rs_copy(k).wait_recv()
        for k in range(1, self.na):
            total = total + self.rs[k]
        self.bx[self.b] = total
        for k in range(1, self.nb):
            self.b_copy(k).start()

    def start_gather(self):
        for k in range(1, self.nb):
            self.b_copy(k).wait_recv()
        total = self.bx[0]
        for k in range(1, self.nb):
            total = total + self.bx[k]
        self.fin[self.a] = total
        for k in range(1, self.na):
            self.g_copy(k).start()

    def finish(self):
        for k in range(1, self.na):
            self.g_copy(k).wait_recv()

    def wait_send(self):
        for k in range(1, self.na):
            self.rs_copy(k).wait_send()
            self.g_copy(k).wait_send()
        for k in range(1, self.nb):
            self.b_copy(k).wait_send()


def kernel(
    vol_hbm, fcot_hbm, ccot_hbm, kf_hbm, kc_hbm,
    fo_ref, co_ref, vg_ref, ffin, cfin,
    raw_v, raw_f, raw_c, kf, kc, st_v, st_f, st_c, st_o, st_co,
    vp, cp, qp, tp, sp, fob, g1, fg, csb, cob, w32, wc32, w32t, wc32n, packed,
    wide_f, wide_t, wide_s, wide_c, band_f, band_t, band_s, band_c, ft, ct,
    frs, fbx, crs, cbx,
    in_sem, hs, hr, know, f_rs_s, f_rs_r, f_b_s, f_b_r, f_g_s, f_g_r,
    c_rs_s, c_rs_r, c_b_s, c_b_r, c_g_s, c_g_r,
):
    gx, gy = lax.axis_index("gx"), lax.axis_index("gy")
    mid = pl.ds(C1, C1)
    barrier = pltpu.get_barrier_semaphore()
    n_halo = 0
    for sx, sy in DIRS:
        near = exists(gx, gy, sx, sy)
        n_halo = n_halo + near.astype(jnp.int32)

        @pl.when(near)
        def _(sx=sx, sy=sy):
            pl.semaphore_signal(
                barrier, inc=1, device_id=(gx + sx, gy + sy), device_id_type=MESH
            )

    loads = [
        pltpu.make_async_copy(src, dst, in_sem.at[i])
        for i, (src, dst) in enumerate(
            (
                (vol_hbm, raw_v), (kf_hbm, kf), (kc_hbm, kc),
                (ccot_hbm, raw_c), (fcot_hbm, raw_f),
            )
        )
    ]
    for load in loads:
        load.start()

    zi, hi = lax.rem(gx, 4), lax.div(gx, 4)
    y_lo, core = lax.div(gy, 2), lax.rem(gy, 2)
    base = hi * 4

    def c_dev_a(d):
        return (base + lax.div(d, 4), lax.rem(d, 4))

    def c_dev_b(d):
        return (d * 4 + zi, gy)

    def f_dev_a(d):
        return (base + lax.div(d, 2), y_lo * 2 + lax.rem(d, 2))

    def f_dev_b(d):
        return (lax.div(d, 2) * 4 + zi, lax.rem(d, 2) * 2 + core)

    a_c, a_f, b_f = zi * 4 + gy, zi * 2 + core, hi * 2 + y_lo

    def spread_word(step):
        reach = 2 << step
        for side, sign in enumerate((1, -1)):

            @pl.when((gx < NGX - reach) if sign == 1 else (gx >= reach))
            def _(side=side, sign=sign):
                pl.semaphore_signal(
                    know.at[step, side], inc=1,
                    device_id=(gx + sign * reach, gy), device_id_type=MESH,
                )

    def hear_word(step):
        reach = 2 << step
        for side, sign in enumerate((1, -1)):

            @pl.when((gx >= reach) if sign == 1 else (gx < NGX - reach))
            def _(side=side):
                pl.semaphore_wait(know.at[step, side], 1)

    vhalo = Halo(vp, mid, 1, D, R, hs.at[0], hr.at[0], gx, gy)
    chalo = Halo(cp, slice(None), 1, HD, HR, hs.at[1], hr.at[1], gx, gy)
    qhalo = Halo(qp, mid, 2, HD, HR, hs.at[2], hr.at[2], gx, gy)
    shalo = Halo(sp, mid, 1, D, R, hs.at[3], hr.at[3], gx, gy)
    f_sum = AllReduce(
        ft, frs, fbx, ffin, (f_rs_s, f_rs_r, f_b_s, f_b_r, f_g_s, f_g_r),
        8, 16, a_f, b_f, f_dev_a, f_dev_b,
    )
    c_sum = AllReduce(
        ct, crs, cbx, cfin, (c_rs_s, c_rs_r, c_b_s, c_b_r, c_g_s, c_g_r),
        16, 8, a_c, hi, c_dev_a, c_dev_b,
    )
    for halo in (vhalo, chalo, qhalo, shalo):
        halo.clear_edges()

    loads[0].wait()
    for t in range(2):
        st_v[t] = raw_v[:, t * 128 : (t + 1) * 128].astype(F32)
    for z in range(D):
        for y in range(R):
            for t in range(2):
                vp[z + 1, y + 1, mid, pl.ds(t * 128, 128)] = st_v[
                    t, pl.ds(z * R + y, C1, stride=D * R), :
                ].astype(BF16)
    pl.semaphore_wait(barrier, n_halo)
    vhalo.start()

    def put_shifts(buf, z, y, order):
        before, after = shifted(buf[z, y, mid, :].astype(F32))
        low, high = (before, after) if order > 0 else (after, before)
        buf[z, y, pl.ds(0, C1), :] = low
        buf[z, y, pl.ds(2 * C1, C1), :] = high

    def own_shifts(buf, h, nz, ny, order):
        @pl.loop(0, nz)
        def _(z):
            for y in range(ny):
                put_shifts(buf, z + h, y + h, order)

    def halo_shifts(buf, h, nz, ny, order):
        @pl.loop(0, h)
        def _(z):
            for y in range(ny + 2 * h):
                put_shifts(buf, z, y, order)
                put_shifts(buf, z + h + nz, y, order)

        @pl.loop(0, nz)
        def _(z):
            for y in range(h):
                put_shifts(buf, z + h, y, order)
                put_shifts(buf, z + h, y + h + ny, order)

    def taps(buf, z, y, back=False):
        rows = []
        for a in range(3):
            for b in range(3):
                da, db = (2 - a, 2 - b) if back else (a, b)
                rows.append(buf[z + da, y + db])
        return jnp.concatenate(rows, axis=0)

    own_shifts(vp, 1, D, R, 1)
    for one in (1, 2):
        loads[one].wait()
    for tap in range(27):
        w32[:, tap * C1 : (tap + 1) * C1] = kf[tap * C1 : (tap + 1) * C1, :].astype(F32)
        wc32[:, tap * C2 : (tap + 1) * C2] = kc[tap * C1 : (tap + 1) * C1, :].astype(F32)

    def eye(n):
        rows = lax.broadcasted_iota(jnp.int32, (n, n), 0)
        return (rows == lax.broadcasted_iota(jnp.int32, (n, n), 1)).astype(F32).astype(BF16)

    wf = w32[...].astype(BF16)
    w32t[...] = dot_nt(eye(C1), kf[...])
    wc32n[...] = dot_nt(eye(C2), kc[...])
    for band in (wide_f, wide_t, wide_s, wide_c):
        band[...] = jnp.zeros(band.shape, F32)
    for a in range(3):
        for r in range(4):
            rows = pl.ds(r * C1, C1)
            wide_f[rows, pl.ds(a * 288 + r * 48, 144)] = w32[:, a * 144 : (a + 1) * 144]
            for b in range(3):
                at = a * 3 + b
                wide_t[rows, pl.ds(a * 288 + (r + 2 - b) * 48, 48)] = w32t[
                    :, at * 48 : (at + 1) * 48
                ]
                wide_s[rows, pl.ds(a * 576 + (r + 2 - b) * 96, 96)] = wc32[
                    :, at * 96 : (at + 1) * 96
                ]
        for r in range(2):
            wide_c[pl.ds(r * C2, C2), pl.ds(a * 192 + r * 48, 144)] = wc32n[
                :, a * 144 : (a + 1) * 144
            ]
    band_f[...] = wide_f[...].astype(BF16)
    band_t[...] = wide_t[...].astype(BF16)
    band_s[...] = wide_s[...].astype(BF16)
    band_c[...] = wide_c[...].astype(BF16)
    packed[...] = jnp.zeros(packed.shape, F32)
    loads[3].wait()
    st_c[...] = raw_c[...].astype(F32)
    for z in range(HD):
        for y in range(HR):
            cp[z + 1, y + 1] = st_c[pl.ds(z * HR + y, C2, stride=HD * HR), :].astype(BF16)
    chalo.start()

    def block(buf, z, y, n):
        return buf[z, pl.ds(y, n)].reshape(n * buf.shape[2], buf.shape[3])

    def fine_band(z, y0):
        four = dot(
            band_f[...], jnp.concatenate([block(vp, z + a, y0, 6) for a in range(3)], axis=0)
        )
        for r in range(4):
            fine_cell(z, y0 + r, four[r * C1 : (r + 1) * C1])

    def fine_row(z, y):
        fine_cell(z, y, dot(wf, taps(vp, z, y)))

    def fine_cell(z, y, pre):
        s = jax.nn.sigmoid(pre)
        out = (vp[z + 1, y + 1, mid, :].astype(F32) + pre * s).astype(BF16)
        g1[z, y] = s * (1.0 + pre * (1.0 - s))
        fob[z, y] = out

    @pl.loop(1, D - 1)
    def _(z):
        for y in range(1, R - 1):
            fine_row(z, y)

    pool_row = lax.broadcasted_iota(jnp.int32, (W, HW), 0)
    pool_col = lax.broadcasted_iota(jnp.int32, (W, HW), 1)
    pool_mat = (lax.div(pool_row, 2) == pool_col).astype(F32).astype(BF16)
    up_row = lax.broadcasted_iota(jnp.int32, (HW, 3 * W), 0)
    up_col = lax.broadcasted_iota(jnp.int32, (HW, 3 * W), 1)
    up_mat = (
        up_row == lax.div(lax.rem(up_col, W), 2) + 1 - lax.div(up_col, W)
    ).astype(F32).astype(BF16)
    loads[4].wait()
    for t in range(2):
        st_f[t] = raw_f[:, t * 128 : (t + 1) * 128].astype(F32)
    vhalo.wait_recv()
    spread_word(0)
    halo_shifts(vp, 1, D, R, 1)

    @pl.loop(0, 2)
    def _(side):
        for y in (0, 4):
            fine_band(side * (D - 1), y)
        for y in (0, R - 1):
            fine_row(side + 1, y)

    @pl.loop(0, HD)
    def _(zc):
        for yc in range(HR):
            four = fob[pl.ds(zc * 2, 2), pl.ds(yc * 2, 2)].reshape(4 * C1, W)
            half = dot(four, pool_mat)
            total = half[0:16] + half[16:32] + half[32:48] + half[48:64]
            qp[zc + 2, yc + 2, mid, :] = (total * 0.125).astype(BF16)

    qhalo.start()
    own_shifts(qp, 2, HD, HR, 1)
    hear_word(0)
    spread_word(1)

    def rows_out(rows, store):
        @pl.loop(0, D)
        def _(z):
            for y in range(R):
                value = rows[z, y].astype(F32)
                for t in range(2):
                    store[t, pl.ds(z * R + y, C1, stride=D * R), :] = value[
                        :, t * 128 : (t + 1) * 128
                    ]

    rows_out(fob, st_o)
    for t in range(2):
        fo_ref[:, t * 128 : (t + 1) * 128] = st_o[t].astype(BF16)
    chalo.wait_recv()
    qhalo.wait_recv()
    hear_word(1)
    spread_word(2)
    halo_shifts(qp, 2, HD, HR, 1)

    @pl.loop(0, HD)
    def _(zp):
        for y0 in range(0, HR + 2, 2):
            two = [
                jnp.concatenate([block(qp, zp * 2 + k + a, y0, 4) for a in range(3)], axis=0)
                for k in range(2)
            ]
            pair = dot(band_c[...], jnp.concatenate(two, axis=1))
            for r in range(2):
                for k in range(2):
                    z, y = zp * 2 + k, y0 + r
                    pre = pair[r * C2 : (r + 1) * C2, k * HW : (k + 1) * HW]
                    s = jax.nn.sigmoid(pre)
                    slope = cp[z, y].astype(F32) * (s * (1.0 + pre * (1.0 - s)))
                    csb[z, y] = slope.astype(BF16)
                    if 1 <= y <= HR:
                        cob[z, y - 1] = (pre * s).astype(BF16)
        for k in range(2):
            z = zp * 2 + k
            wide = dot(csb[z].reshape((HR + 2) * C2, HW), up_mat).astype(BF16)
            for c in range(3):
                tp[z, :, pl.ds(c * C2, C2), :] = wide[:, c * W : (c + 1) * W].reshape(
                    HR + 2, C2, W
                )

    def across(rows):
        rows = jnp.concatenate([rows, jnp.zeros((80, rows.shape[1]), F32)], axis=0)
        return jnp.transpose(rows)

    cells = [(z + 1, y + 1) for z in range(HD) for y in range(HR)]
    ck = dot_nt(
        jnp.concatenate([taps(qp, *at) for at in cells], axis=1),
        jnp.concatenate([csb[at] for at in cells], axis=1),
    )
    ck = across(ck)
    for i in range(4):
        for t in range(4):
            ct[i * 4 + t] = ck[i * 8 : (i + 1) * 8, t * 128 : (t + 1) * 128]
    c_sum.start_scatter()

    @pl.loop(0, HD)
    def _(zc):
        four = dot(
            band_s[...], jnp.concatenate([block(tp, zc + 2 - a, 0, 6) for a in range(3)], axis=0)
        )
        for yc in range(HR):
            spread = four[yc * C1 : (yc + 1) * C1] * 0.125
            for zz in range(2):
                for yy in range(2):
                    z, y = zc * 2 + zz, yc * 2 + yy
                    cot = jnp.concatenate(
                        [st_f[t, pl.ds(z * R + y, C1, stride=D * R), :] for t in range(2)], axis=1
                    )
                    grad = cot + spread
                    fg[z, y] = grad
                    sp[z + 1, y + 1, mid, :] = (grad * g1[z, y]).astype(BF16)

    shalo.start()
    hear_word(2)
    spread_word(3)

    def slope_rows(z, yb):
        if not 0 <= z < D:
            return jnp.zeros((4 * C1, W), BF16)
        return sp[z + 1, pl.ds(yb * 4 + 1, 4), mid, :].reshape(4 * C1, W)

    steps = [(z, yb) for z in range(D + 2) for yb in range(2)]
    pairs = dot_nt(
        jnp.concatenate([block(vp, z, yb * 4, 6) for z, yb in steps], axis=1),
        jnp.concatenate(
            [
                jnp.concatenate([slope_rows(z - a, yb) for a in range(3)], axis=0)
                for z, yb in steps
            ],
            axis=1,
        ),
    )
    pairs = jnp.concatenate([pairs, jnp.zeros((288, 64), F32)], axis=1)
    pairs = jnp.transpose(jnp.concatenate([pairs, jnp.zeros((96, 256), F32)], axis=0))
    for a in range(3):
        total = pairs[a * 64 : a * 64 + 16, 0:144]
        for y in range(1, 4):
            total = total + pairs[a * 64 + y * 16 : a * 64 + y * 16 + 16, y * 48 : y * 48 + 144]
        packed[:, a * 144 : (a + 1) * 144] = total
    fk = packed[...]
    for i in range(2):
        for t in range(4):
            ft[i * 4 + t] = fk[i * 8 : (i + 1) * 8, t * 128 : (t + 1) * 128]
    f_sum.start_scatter()
    hear_word(3)
    c_sum.start_exchange()
    own_shifts(sp, 1, D, R, -1)
    f_sum.start_exchange()
    shalo.wait_recv()
    halo_shifts(sp, 1, D, R, -1)

    @pl.loop(0, D)
    def _(z):
        for y0 in (0, 4):
            four = dot(
                band_t[...],
                jnp.concatenate([block(sp, z + 2 - a, y0, 6) for a in range(3)], axis=0),
            )
            for r in range(4):
                fg[z, y0 + r] = fg[z, y0 + r] + four[r * C1 : (r + 1) * C1]

    c_sum.start_gather()
    f_sum.start_gather()
    rows_out(fg, st_o)
    for t in range(2):
        vg_ref[:, t * 128 : (t + 1) * 128] = st_o[t].astype(BF16)
    for z in range(HD):
        for y in range(HR):
            st_co[pl.ds(z * HR + y, C2, stride=HD * HR), :] = cob[z + 1, y].astype(F32)
    co_ref[...] = st_co[...].astype(BF16)
    for one in (vhalo, chalo, qhalo, shalo, c_sum, f_sum):
        one.wait_send()
    c_sum.finish()
    f_sum.finish()


def emit_kernel(fo, co, vg, ffin, cfin, fo_hbm, co_hbm, vg_hbm, fk_hbm, ck_hbm, fk, ck, sem):
    copies = [
        pltpu.make_async_copy(src, dst, sem.at[i])
        for i, (src, dst) in enumerate(
            ((fo, fo_hbm), (vg, vg_hbm), (co, co_hbm), (fk, fk_hbm), (ck, ck_hbm))
        )
    ]
    for i in range(3):
        copies[i].start()
    for i in range(2):
        for t in range(4):
            tile = ffin[i * 4 + t] * (1048576.0**-0.5)
            for k in range(8):
                tap = t * 8 + k
                if tap < 27:
                    fk[tap, pl.ds(i * 8, 8), :] = tile[:, k * C1 : (k + 1) * C1]
    copies[3].start()
    for t in range(4):
        rows = jnp.concatenate([cfin[i * 4 + t] for i in range(4)], axis=0)
        cols = jnp.transpose(rows * (131072.0**-0.5))
        for k in range(8):
            tap = t * 8 + k
            if tap < 27:
                ck[tap] = cols[k * C1 : (k + 1) * C1, :]
    copies[4].start()
    for one in copies:
        one.wait()


def local(volume, fine_kernel, coarse_kernel, fine_cotangent, coarse_cotangent):
    kf = fine_kernel.reshape(27 * C1, C1)
    kc = coarse_kernel.transpose(0, 1, 2, 4, 3).reshape(27 * C1, C2)
    hbm = pl.BlockSpec(memory_space=pltpu.HBM)
    vmem = pl.BlockSpec(memory_space=pltpu.VMEM)
    dma = pltpu.SemaphoreType.DMA
    V = pltpu.VMEM
    tile = (8, 128)
    fine, coarse = (C1 * D * R, W), (C2 * HD * HR, HW)
    parts = pl.pallas_call(
        kernel,
        out_shape=[
            jax.ShapeDtypeStruct(fine, BF16),
            jax.ShapeDtypeStruct(coarse, BF16),
            jax.ShapeDtypeStruct(fine, BF16),
            jax.ShapeDtypeStruct((8, *tile), F32),
            jax.ShapeDtypeStruct((16, *tile), F32),
        ],
        in_specs=[hbm] * 5,
        out_specs=[vmem] * 5,
        scratch_shapes=[
            V(fine, BF16), V(fine, BF16), V(coarse, BF16),
            V((27 * C1, C1), BF16), V((27 * C1, C2), BF16),
            V((2, C1 * D * R, 128), F32), V((2, C1 * D * R, 128), F32), V(coarse, F32),
            V((2, C1 * D * R, 128), F32), V(coarse, F32),
            V((D + 2, R + 2, 3 * C1, W), BF16),
            V((HD + 2, HR + 2, C2, HW), BF16),
            V((HD + 4, HR + 4, 3 * C1, HW), BF16),
            V((HD + 2, HR + 2, 3 * C2, W), BF16),
            V((D + 2, R + 2, 3 * C1, W), BF16),
            V((D, R, C1, W), BF16), V((D, R, C1, W), F32), V((D, R, C1, W), F32),
            V((HD + 2, HR + 2, C2, HW), BF16), V((HD + 2, HR, C2, HW), BF16),
            V((C1, 27 * C1), F32), V((C1, 27 * C2), F32),
            V((C1, 27 * C1), F32), V((C2, 27 * C1), F32), V((C1, 512), F32),
            V((64, 864), F32), V((64, 864), F32), V((64, 1728), F32), V((64, 576), F32),
            V((64, 864), BF16), V((64, 864), BF16), V((64, 1728), BF16), V((64, 576), BF16),
            V((8, *tile), F32), V((16, *tile), F32),
            V((8, *tile), F32), V((16, *tile), F32),
            V((16, *tile), F32), V((8, *tile), F32),
            dma((5,)), dma((4, 8)), dma((4, 8)), pltpu.SemaphoreType.REGULAR((4, 2)),
            dma((8,)), dma((8,)), dma((16,)), dma((16,)), dma((8,)), dma((8,)),
            dma((16,)), dma((16,)), dma((8,)), dma((8,)), dma((16,)), dma((16,)),
        ],
        compiler_params=pltpu.CompilerParams(
            collective_id=0, has_side_effects=True, vmem_limit_bytes=48 << 20
        ),
        name="unet_levels",
    )(
        *(
            pltpu.with_memory_space_constraint(value, pltpu.HBM)
            for value in (
                volume.reshape(fine), fine_cotangent.reshape(fine),
                coarse_cotangent.reshape(coarse), kf, kc,
            )
        )
    )
    fo, co, vg, fk, ck = pl.pallas_call(
        emit_kernel,
        out_shape=[
            jax.ShapeDtypeStruct(fine, BF16),
            jax.ShapeDtypeStruct(coarse, BF16),
            jax.ShapeDtypeStruct(fine, BF16),
            jax.ShapeDtypeStruct((27, C1, C1), F32),
            jax.ShapeDtypeStruct((27, C1, C2), F32),
        ],
        in_specs=[vmem] * 5,
        out_specs=[hbm] * 5,
        scratch_shapes=[V((27, C1, C1), F32), V((27, C1, C2), F32), dma((5,))],
        compiler_params=pltpu.CompilerParams(vmem_limit_bytes=8 << 20),
        name="emit",
    )(*parts)
    return (
        fo.reshape(volume.shape),
        co.reshape(coarse_cotangent.shape),
        vg.reshape(volume.shape),
        fk.reshape(fine_kernel.shape),
        ck.reshape(3, 3, 3, C1, C2).transpose(0, 1, 2, 4, 3),
    )


def solution(mesh):
    block = P(None, "gx", "gy", None)
    return jax.shard_map(
        local,
        mesh=mesh,
        in_specs=(block, P(), P(), block, block),
        out_specs=(block, block, block, P(), P()),
        check_vma=False,
    )
```

```python
import jax
import jax.numpy as jnp
from jax import lax
from jax.experimental import pallas as pl
from jax.experimental.pallas import tpu as pltpu
from jax.sharding import PartitionSpec as P

F32 = jnp.float32
BF16 = jnp.bfloat16
MESH = pl.DeviceIdType.MESH
C1, C2 = 16, 32
D, R, W = 4, 8, 256
HD, HR, HW = 2, 4, 128
NGX, NGY = 32, 4
DIRS = [(-1, -1), (-1, 1), (1, -1), (1, 1), (-1, 0), (1, 0), (0, -1), (0, 1)]
NT = (((1,), (1,)), ((), ()))


def dot(a, b):
    return jnp.dot(a, b, preferred_element_type=F32)


def dot_nt(a, b):
    return lax.dot_general(a, b, NT, preferred_element_type=F32)


def shifted(x):
    n = x.shape[1]
    lane = lax.broadcasted_iota(jnp.int32, x.shape, 1)
    before = jnp.where(lane == 0, 0.0, pltpu.roll(x, 1, axis=1))
    after = jnp.where(lane == n - 1, 0.0, pltpu.roll(x, n - 1, axis=1))
    return before.astype(BF16), after.astype(BF16)


def exists(gx, gy, sx, sy):
    cond = None
    for ok in (
        [gx < NGX - 1] if sx == 1 else [gx > 0] if sx == -1 else []
    ) + ([gy < NGY - 1] if sy == 1 else [gy > 0] if sy == -1 else []):
        cond = ok if cond is None else jnp.logical_and(cond, ok)
    return cond


def span(s, h, n, sending):
    if s == 0:
        return h, n
    if sending:
        return (n, h) if s == 1 else (h, h)
    return (0, h) if s == 1 else (h + n, h)


class Halo:
    def __init__(self, buf, chan, h, nz, ny, send_sem, recv_sem, gx, gy):
        self.buf, self.chan, self.h, self.nz, self.ny = buf, chan, h, nz, ny
        self.send_sem, self.recv_sem, self.gx, self.gy = send_sem, recv_sem, gx, gy

    def part(self, sx, sy, sending):
        z0, zn = span(sx, self.h, self.nz, sending)
        y0, yn = span(sy, self.h, self.ny, sending)
        return self.buf.at[pl.ds(z0, zn), pl.ds(y0, yn), self.chan, :]

    def desc(self, i):
        sx, sy = DIRS[i]
        return pltpu.make_async_remote_copy(
            src_ref=self.part(sx, sy, True),
            dst_ref=self.part(sx, sy, False),
            send_sem=self.send_sem.at[i],
            recv_sem=self.recv_sem.at[i],
            device_id=(self.gx + sx, self.gy + sy),
            device_id_type=MESH,
        )

    def clear_edges(self):
        h, nz, ny = self.h, self.nz, self.ny
        for s, n, axis, g, last in (
            (-1, nz, 0, self.gx, 0),
            (1, nz, 0, self.gx, NGX - 1),
            (-1, ny, 1, self.gy, 0),
            (1, ny, 1, self.gy, NGY - 1),
        ):
            at = 0 if s == -1 else h + n
            rows = pl.ds(at, h)

            @pl.when(g == last)
            def _(axis=axis, rows=rows):
                index = (rows, slice(None)) if axis == 0 else (slice(None), rows)
                view = self.buf.at[(*index, self.chan, slice(None))]
                view[...] = jnp.zeros(view.shape, view.dtype)

    def start(self):
        for i, (sx, sy) in enumerate(DIRS):

            @pl.when(exists(self.gx, self.gy, sx, sy))
            def _(i=i):
                self.desc(i).start()

    def wait_recv(self, chosen=range(8)):
        for i in chosen:
            sx, sy = DIRS[i]

            @pl.when(exists(self.gx, self.gy, -sx, -sy))
            def _(i=i):
                self.desc(i).wait_recv()

    def wait_send(self):
        for i, (sx, sy) in enumerate(DIRS):

            @pl.when(exists(self.gx, self.gy, sx, sy))
            def _(i=i):
                self.desc(i).wait_send()


class PlaneHalo(Halo):
    def plane(self, p, i):
        sx, sy = DIRS[i]
        y0, yn = span(sy, self.h, self.ny, True)
        y1, _ = span(sy, self.h, self.ny, False)
        return pltpu.make_async_remote_copy(
            src_ref=self.buf.at[pl.ds(p + self.h, 1), pl.ds(y0, yn), self.chan, :],
            dst_ref=self.buf.at[pl.ds(p + self.h - 2 * sx, 1), pl.ds(y1, yn), self.chan, :],
            send_sem=self.send_sem.at[p, i],
            recv_sem=self.recv_sem.at[p, i],
            device_id=(self.gx + sx, self.gy + sy),
            device_id_type=MESH,
        )

    def start(self, p):
        for i, (sx, sy) in enumerate(DIRS):

            @pl.when(exists(self.gx, self.gy, sx, sy))
            def _(i=i):
                self.plane(p, i).start()

    def wait_recv(self):
        for i, (sx, sy) in enumerate(DIRS):

            @pl.when(exists(self.gx, self.gy, -sx, -sy))
            def _(i=i):
                for p in range(2):
                    self.plane(p, i).wait_recv()

    def wait_send(self):
        for i, (sx, sy) in enumerate(DIRS):

            @pl.when(exists(self.gx, self.gy, sx, sy))
            def _(i=i):
                for p in range(2):
                    self.plane(p, i).wait_send()


class AllReduce:
    def __init__(self, terms, rs, bx, fin, sems, na, nb, a, b, dev_a, dev_b):
        self.terms, self.rs, self.bx, self.fin = terms, rs, bx, fin
        self.na, self.nb, self.a, self.b = na, nb, a, b
        self.dev_a, self.dev_b = dev_a, dev_b
        self.rs_s, self.rs_r, self.b_s, self.b_r, self.g_s, self.g_r = sems

    def rs_copy(self, k):
        d = lax.rem(self.a + k, self.na)
        return pltpu.make_async_remote_copy(
            self.terms.at[d], self.rs.at[k], self.rs_s.at[k], self.rs_r.at[k], self.dev_a(d), MESH
        )

    def b_copy(self, k):
        d = lax.rem(self.b + k, self.nb)
        return pltpu.make_async_remote_copy(
            self.bx.at[self.b], self.bx.at[self.b], self.b_s.at[k], self.b_r.at[k], self.dev_b(d), MESH
        )

    def g_copy(self, k):
        d = lax.rem(self.a + k, self.na)
        return pltpu.make_async_remote_copy(
            self.fin.at[self.a], self.fin.at[self.a], self.g_s.at[k], self.g_r.at[k], self.dev_a(d), MESH
        )

    def start_scatter(self):
        for k in range(1, self.na):
            self.rs_copy(k).start()

    def start_exchange(self):
        total = self.terms[self.a]
        for k in range(1, self.na):
            self.rs_copy(k).wait_recv()
        for k in range(1, self.na):
            total = total + self.rs[k]
        self.bx[self.b] = total
        for k in range(1, self.nb):
            self.b_copy(k).start()

    def start_gather(self):
        for k in range(1, self.nb):
            self.b_copy(k).wait_recv()
        total = self.bx[0]
        for k in range(1, self.nb):
            total = total + self.bx[k]
        self.fin[self.a] = total
        for k in range(1, self.na):
            self.g_copy(k).start()

    def finish(self):
        for k in range(1, self.na):
            self.g_copy(k).wait_recv()

    def wait_send(self):
        for k in range(1, self.na):
            self.rs_copy(k).wait_send()
            self.g_copy(k).wait_send()
        for k in range(1, self.nb):
            self.b_copy(k).wait_send()


def kernel(
    vol_hbm, fcot_hbm, ccot_hbm, kf_hbm, kc_hbm,
    fo_ref, co_ref, vg_ref, ffin, cfin,
    raw_v, raw_f, raw_c, kf, kc, st_v, st_f, st_c, st_o, st_co,
    vp, cp, qp, tp, sp, fob, g1, fg, csb, cob, w32, wc32, w32t, wc32n, packed,
    wide_f, wide_t, wide_s, wide_c, band_f, band_t, band_s, band_c, ft, ct,
    frs, fbx, crs, cbx,
    in_sem, hs, hr, qs, qr, know, f_rs_s, f_rs_r, f_b_s, f_b_r, f_g_s, f_g_r,
    c_rs_s, c_rs_r, c_b_s, c_b_r, c_g_s, c_g_r,
):
    gx, gy = lax.axis_index("gx"), lax.axis_index("gy")
    mid = pl.ds(C1, C1)
    barrier = pltpu.get_barrier_semaphore()
    n_halo = 0
    for sx, sy in DIRS:
        near = exists(gx, gy, sx, sy)
        n_halo = n_halo + near.astype(jnp.int32)

        @pl.when(near)
        def _(sx=sx, sy=sy):
            pl.semaphore_signal(
                barrier, inc=1, device_id=(gx + sx, gy + sy), device_id_type=MESH
            )

    zi, hi = lax.rem(gx, 4), lax.div(gx, 4)
    ring = [lax.div(hi, 4) * 16 + lax.rem(hi + k, 4) * 4 + zi for k in (1, 3)]
    across = lax.rem(gx + 16, NGX)
    for far in (*ring, across):
        pl.semaphore_signal(barrier, inc=1, device_id=(far, gy), device_id_type=MESH)

    def tell(one, device):
        pl.semaphore_signal(know.at[one], inc=1, device_id=(device, gy), device_id_type=MESH)

    loads = [
        pltpu.make_async_copy(src, dst, in_sem.at[i])
        for i, (src, dst) in enumerate(
            (
                (vol_hbm, raw_v), (kf_hbm, kf), (kc_hbm, kc),
                (ccot_hbm, raw_c), (fcot_hbm, raw_f),
            )
        )
    ]
    for load in loads:
        load.start()

    y_lo, core = lax.div(gy, 2), lax.rem(gy, 2)
    base = hi * 4

    def c_dev_a(d):
        return (base + lax.div(d, 4), lax.rem(d, 4))

    def c_dev_b(d):
        return (d * 4 + zi, gy)

    def f_dev_a(d):
        return (base + lax.div(d, 2), y_lo * 2 + lax.rem(d, 2))

    def f_dev_b(d):
        return (lax.div(d, 2) * 4 + zi, lax.rem(d, 2) * 2 + core)

    a_c, a_f, b_f = zi * 4 + gy, zi * 2 + core, hi * 2 + y_lo

    def hear_ring():
        for one in range(2):
            pl.semaphore_wait(know.at[one], 1)
        tell(2, across)

    def hear_across():
        pl.semaphore_wait(know.at[2], 1)

    vhalo = Halo(vp, mid, 1, D, R, hs.at[0], hr.at[0], gx, gy)
    chalo = Halo(cp, slice(None), 1, HD, HR, hs.at[1], hr.at[1], gx, gy)
    qhalo = PlaneHalo(qp, mid, 2, HD, HR, qs, qr, gx, gy)
    shalo = Halo(sp, mid, 1, D, R, hs.at[3], hr.at[3], gx, gy)
    f_sum = AllReduce(
        ft, frs, fbx, ffin, (f_rs_s, f_rs_r, f_b_s, f_b_r, f_g_s, f_g_r),
        8, 16, a_f, b_f, f_dev_a, f_dev_b,
    )
    c_sum = AllReduce(
        ct, crs, cbx, cfin, (c_rs_s, c_rs_r, c_b_s, c_b_r, c_g_s, c_g_r),
        16, 8, a_c, hi, c_dev_a, c_dev_b,
    )
    for halo in (vhalo, chalo, qhalo, shalo):
        halo.clear_edges()

    loads[0].wait()
    for t in range(2):
        st_v[t] = raw_v[:, t * 128 : (t + 1) * 128].astype(F32)
    for z in range(D):
        for y in range(R):
            for t in range(2):
                vp[z + 1, y + 1, mid, pl.ds(t * 128, 128)] = st_v[
                    t, pl.ds(z * R + y, C1, stride=D * R), :
                ].astype(BF16)
    pl.semaphore_wait(barrier, n_halo + 3)
    vhalo.start()
    for one in range(2):
        tell(one, ring[one])

    def put_shifts(buf, z, y, order):
        before, after = shifted(buf[z, y, mid, :].astype(F32))
        low, high = (before, after) if order > 0 else (after, before)
        buf[z, y, pl.ds(0, C1), :] = low
        buf[z, y, pl.ds(2 * C1, C1), :] = high

    def own_shifts(buf, h, nz, ny, order):
        @pl.loop(0, nz)
        def _(z):
            for y in range(ny):
                put_shifts(buf, z + h, y + h, order)

    def halo_shifts(buf, h, nz, ny, order):
        @pl.loop(0, h)
        def _(z):
            for y in range(ny + 2 * h):
                put_shifts(buf, z, y, order)
                put_shifts(buf, z + h + nz, y, order)

        @pl.loop(0, nz)
        def _(z):
            for y in range(h):
                put_shifts(buf, z + h, y, order)
                put_shifts(buf, z + h, y + h + ny, order)

    def taps(buf, z, y, back=False):
        rows = []
        for a in range(3):
            for b in range(3):
                da, db = (2 - a, 2 - b) if back else (a, b)
                rows.append(buf[z + da, y + db])
        return jnp.concatenate(rows, axis=0)

    own_shifts(vp, 1, D, R, 1)
    for one in (1, 2):
        loads[one].wait()
    for tap in range(27):
        w32[:, tap * C1 : (tap + 1) * C1] = kf[tap * C1 : (tap + 1) * C1, :].astype(F32)
        wc32[:, tap * C2 : (tap + 1) * C2] = kc[tap * C1 : (tap + 1) * C1, :].astype(F32)

    def eye(n):
        rows = lax.broadcasted_iota(jnp.int32, (n, n), 0)
        return (rows == lax.broadcasted_iota(jnp.int32, (n, n), 1)).astype(F32).astype(BF16)

    wf = w32[...].astype(BF16)
    w32t[...] = dot_nt(eye(C1), kf[...])
    wc32n[...] = dot_nt(eye(C2), kc[...])
    for band in (wide_f, wide_t, wide_s, wide_c):
        band[...] = jnp.zeros(band.shape, F32)
    for a in range(3):
        for r in range(4):
            rows = pl.ds(r * C1, C1)
            wide_f[rows, pl.ds(a * 288 + r * 48, 144)] = w32[:, a * 144 : (a + 1) * 144]
            for b in range(3):
                at = a * 3 + b
                wide_t[rows, pl.ds(a * 288 + (r + 2 - b) * 48, 48)] = w32t[
                    :, at * 48 : (at + 1) * 48
                ]
                wide_s[rows, pl.ds(a * 576 + (r + 2 - b) * 96, 96)] = wc32[
                    :, at * 96 : (at + 1) * 96
                ]
        for r in range(2):
            wide_c[pl.ds(r * C2, C2), pl.ds(a * 192 + r * 48, 144)] = wc32n[
                :, a * 144 : (a + 1) * 144
            ]
    band_f[...] = wide_f[...].astype(BF16)
    band_t[...] = wide_t[...].astype(BF16)
    band_s[...] = wide_s[...].astype(BF16)
    band_c[...] = wide_c[...].astype(BF16)
    packed[...] = jnp.zeros(packed.shape, F32)
    loads[3].wait()
    st_c[...] = raw_c[...].astype(F32)
    for z in range(HD):
        for y in range(HR):
            cp[z + 1, y + 1] = st_c[pl.ds(z * HR + y, C2, stride=HD * HR), :].astype(BF16)
    chalo.start()

    def block(buf, z, y, n):
        return buf[z, pl.ds(y, n)].reshape(n * buf.shape[2], buf.shape[3])

    def fine_band(z, y0):
        four = dot(
            band_f[...], jnp.concatenate([block(vp, z + a, y0, 6) for a in range(3)], axis=0)
        )
        for r in range(4):
            fine_cell(z, y0 + r, four[r * C1 : (r + 1) * C1])

    def fine_row(z, y):
        fine_cell(z, y, dot(wf, taps(vp, z, y)))

    def fine_cell(z, y, pre):
        s = jax.nn.sigmoid(pre)
        out = (vp[z + 1, y + 1, mid, :].astype(F32) + pre * s).astype(BF16)
        g1[z, y] = s * (1.0 + pre * (1.0 - s))
        fob[z, y] = out

    @pl.loop(1, D - 1)
    def _(z):
        for y in range(1, R - 1):
            fine_row(z, y)

    pool_row = lax.broadcasted_iota(jnp.int32, (W, HW), 0)
    pool_col = lax.broadcasted_iota(jnp.int32, (W, HW), 1)
    pool_mat = (lax.div(pool_row, 2) == pool_col).astype(F32).astype(BF16)
    up_row = lax.broadcasted_iota(jnp.int32, (HW, 3 * W), 0)
    up_col = lax.broadcasted_iota(jnp.int32, (HW, 3 * W), 1)
    up_mat = (
        up_row == lax.div(lax.rem(up_col, W), 2) + 1 - lax.div(up_col, W)
    ).astype(F32).astype(BF16)
    loads[4].wait()
    for t in range(2):
        st_f[t] = raw_f[:, t * 128 : (t + 1) * 128].astype(F32)
    vhalo.wait_recv((6, 7))

    @pl.loop(0, D)
    def _(z):
        for y in (0, R + 1):
            put_shifts(vp, z + 1, y, 1)

    late = (zi == 0).astype(jnp.int32)
    for side in (late, 1 - late):

        @pl.when(side == 0)
        def _():
            vhalo.wait_recv((2, 3, 5))

        @pl.when(side == 1)
        def _():
            vhalo.wait_recv((0, 1, 4))

        for y in range(R + 2):
            put_shifts(vp, side * (D + 1), y, 1)
        for y in (0, 4):
            fine_band(side * (D - 1), y)
        for y in (0, R - 1):
            fine_row(side + 1, y)
        for yc in range(HR):
            four = fob[pl.ds(side * 2, 2), pl.ds(yc * 2, 2)].reshape(4 * C1, W)
            half = dot(four, pool_mat)
            total = half[0:16] + half[16:32] + half[32:48] + half[48:64]
            qp[side + 2, yc + 2, mid, :] = (total * 0.125).astype(BF16)
        qhalo.start(side)

    hear_ring()
    own_shifts(qp, 2, HD, HR, 1)

    def rows_out(rows, store):
        @pl.loop(0, D)
        def _(z):
            for y in range(R):
                value = rows[z, y].astype(F32)
                for t in range(2):
                    store[t, pl.ds(z * R + y, C1, stride=D * R), :] = value[
                        :, t * 128 : (t + 1) * 128
                    ]

    rows_out(fob, st_o)
    for t in range(2):
        fo_ref[:, t * 128 : (t + 1) * 128] = st_o[t].astype(BF16)
    chalo.wait_recv()
    qhalo.wait_recv()
    hear_across()
    halo_shifts(qp, 2, HD, HR, 1)

    @pl.loop(0, HD)
    def _(zp):
        for y0 in range(0, HR + 2, 2):
            two = [
                jnp.concatenate([block(qp, zp * 2 + k + a, y0, 4) for a in range(3)], axis=0)
                for k in range(2)
            ]
            pair = dot(band_c[...], jnp.concatenate(two, axis=1))
            for r in range(2):
                for k in range(2):
                    z, y = zp * 2 + k, y0 + r
                    pre = pair[r * C2 : (r + 1) * C2, k * HW : (k + 1) * HW]
                    s = jax.nn.sigmoid(pre)
                    slope = cp[z, y].astype(F32) * (s * (1.0 + pre * (1.0 - s)))
                    csb[z, y] = slope.astype(BF16)
                    if 1 <= y <= HR:
                        cob[z, y - 1] = (pre * s).astype(BF16)
        for k in range(2):
            z = zp * 2 + k
            wide = dot(csb[z].reshape((HR + 2) * C2, HW), up_mat).astype(BF16)
            for c in range(3):
                tp[z, :, pl.ds(c * C2, C2), :] = wide[:, c * W : (c + 1) * W].reshape(
                    HR + 2, C2, W
                )

    def turned(rows):
        rows = jnp.concatenate([rows, jnp.zeros((80, rows.shape[1]), F32)], axis=0)
        return jnp.transpose(rows)

    cells = [(z + 1, y + 1) for z in range(HD) for y in range(HR)]
    ck = dot_nt(
        jnp.concatenate([taps(qp, *at) for at in cells], axis=1),
        jnp.concatenate([csb[at] for at in cells], axis=1),
    )
    ck = turned(ck)
    for i in range(4):
        for t in range(4):
            ct[i * 4 + t] = ck[i * 8 : (i + 1) * 8, t * 128 : (t + 1) * 128]
    c_sum.start_scatter()

    @pl.loop(0, HD)
    def _(zc):
        four = dot(
            band_s[...], jnp.concatenate([block(tp, zc + 2 - a, 0, 6) for a in range(3)], axis=0)
        )
        for yc in range(HR):
            spread = four[yc * C1 : (yc + 1) * C1] * 0.125
            for zz in range(2):
                for yy in range(2):
                    z, y = zc * 2 + zz, yc * 2 + yy
                    cot = jnp.concatenate(
                        [st_f[t, pl.ds(z * R + y, C1, stride=D * R), :] for t in range(2)], axis=1
                    )
                    grad = cot + spread
                    fg[z, y] = grad
                    sp[z + 1, y + 1, mid, :] = (grad * g1[z, y]).astype(BF16)

    shalo.start()

    def slope_rows(z, yb):
        if not 0 <= z < D:
            return jnp.zeros((4 * C1, W), BF16)
        return sp[z + 1, pl.ds(yb * 4 + 1, 4), mid, :].reshape(4 * C1, W)

    steps = [(z, yb) for z in range(D + 2) for yb in range(2)]
    pairs = dot_nt(
        jnp.concatenate([block(vp, z, yb * 4, 6) for z, yb in steps], axis=1),
        jnp.concatenate(
            [
                jnp.concatenate([slope_rows(z - a, yb) for a in range(3)], axis=0)
                for z, yb in steps
            ],
            axis=1,
        ),
    )
    pairs = jnp.concatenate([pairs, jnp.zeros((288, 64), F32)], axis=1)
    pairs = jnp.transpose(jnp.concatenate([pairs, jnp.zeros((96, 256), F32)], axis=0))
    for a in range(3):
        total = pairs[a * 64 : a * 64 + 16, 0:144]
        for y in range(1, 4):
            total = total + pairs[a * 64 + y * 16 : a * 64 + y * 16 + 16, y * 48 : y * 48 + 144]
        packed[:, a * 144 : (a + 1) * 144] = total
    fk = packed[...]
    for i in range(2):
        for t in range(4):
            ft[i * 4 + t] = fk[i * 8 : (i + 1) * 8, t * 128 : (t + 1) * 128]
    f_sum.start_scatter()
    c_sum.start_exchange()
    own_shifts(sp, 1, D, R, -1)
    f_sum.start_exchange()
    shalo.wait_recv()
    halo_shifts(sp, 1, D, R, -1)

    @pl.loop(0, D)
    def _(z):
        for y0 in (0, 4):
            four = dot(
                band_t[...],
                jnp.concatenate([block(sp, z + 2 - a, y0, 6) for a in range(3)], axis=0),
            )
            for r in range(4):
                fg[z, y0 + r] = fg[z, y0 + r] + four[r * C1 : (r + 1) * C1]

    c_sum.start_gather()
    f_sum.start_gather()
    rows_out(fg, st_o)
    for t in range(2):
        vg_ref[:, t * 128 : (t + 1) * 128] = st_o[t].astype(BF16)
    for z in range(HD):
        for y in range(HR):
            st_co[pl.ds(z * HR + y, C2, stride=HD * HR), :] = cob[z + 1, y].astype(F32)
    co_ref[...] = st_co[...].astype(BF16)
    for one in (vhalo, chalo, qhalo, shalo, c_sum, f_sum):
        one.wait_send()
    c_sum.finish()
    f_sum.finish()


def emit_kernel(fo, co, vg, ffin, cfin, fo_hbm, co_hbm, vg_hbm, fk_hbm, ck_hbm, fk, ck, sem):
    copies = [
        pltpu.make_async_copy(src, dst, sem.at[i])
        for i, (src, dst) in enumerate(
            ((fo, fo_hbm), (vg, vg_hbm), (co, co_hbm), (fk, fk_hbm), (ck, ck_hbm))
        )
    ]
    for i in range(3):
        copies[i].start()
    for i in range(2):
        for t in range(4):
            tile = ffin[i * 4 + t] * (1048576.0**-0.5)
            for k in range(8):
                tap = t * 8 + k
                if tap < 27:
                    fk[tap, pl.ds(i * 8, 8), :] = tile[:, k * C1 : (k + 1) * C1]
    copies[3].start()
    for t in range(4):
        rows = jnp.concatenate([cfin[i * 4 + t] for i in range(4)], axis=0)
        cols = jnp.transpose(rows * (131072.0**-0.5))
        for k in range(8):
            tap = t * 8 + k
            if tap < 27:
                ck[tap] = cols[k * C1 : (k + 1) * C1, :]
    copies[4].start()
    for one in copies:
        one.wait()


def local(volume, fine_kernel, coarse_kernel, fine_cotangent, coarse_cotangent):
    kf = fine_kernel.reshape(27 * C1, C1)
    kc = coarse_kernel.transpose(0, 1, 2, 4, 3).reshape(27 * C1, C2)
    hbm = pl.BlockSpec(memory_space=pltpu.HBM)
    vmem = pl.BlockSpec(memory_space=pltpu.VMEM)
    dma = pltpu.SemaphoreType.DMA
    V = pltpu.VMEM
    tile = (8, 128)
    fine, coarse = (C1 * D * R, W), (C2 * HD * HR, HW)
    parts = pl.pallas_call(
        kernel,
        out_shape=[
            jax.ShapeDtypeStruct(fine, BF16),
            jax.ShapeDtypeStruct(coarse, BF16),
            jax.ShapeDtypeStruct(fine, BF16),
            jax.ShapeDtypeStruct((8, *tile), F32),
            jax.ShapeDtypeStruct((16, *tile), F32),
        ],
        in_specs=[hbm] * 5,
        out_specs=[vmem] * 5,
        scratch_shapes=[
            V(fine, BF16), V(fine, BF16), V(coarse, BF16),
            V((27 * C1, C1), BF16), V((27 * C1, C2), BF16),
            V((2, C1 * D * R, 128), F32), V((2, C1 * D * R, 128), F32), V(coarse, F32),
            V((2, C1 * D * R, 128), F32), V(coarse, F32),
            V((D + 2, R + 2, 3 * C1, W), BF16),
            V((HD + 2, HR + 2, C2, HW), BF16),
            V((HD + 4, HR + 4, 3 * C1, HW), BF16),
            V((HD + 2, HR + 2, 3 * C2, W), BF16),
            V((D + 2, R + 2, 3 * C1, W), BF16),
            V((D, R, C1, W), BF16), V((D, R, C1, W), F32), V((D, R, C1, W), F32),
            V((HD + 2, HR + 2, C2, HW), BF16), V((HD + 2, HR, C2, HW), BF16),
            V((C1, 27 * C1), F32), V((C1, 27 * C2), F32),
            V((C1, 27 * C1), F32), V((C2, 27 * C1), F32), V((C1, 512), F32),
            V((64, 864), F32), V((64, 864), F32), V((64, 1728), F32), V((64, 576), F32),
            V((64, 864), BF16), V((64, 864), BF16), V((64, 1728), BF16), V((64, 576), BF16),
            V((8, *tile), F32), V((16, *tile), F32),
            V((8, *tile), F32), V((16, *tile), F32),
            V((16, *tile), F32), V((8, *tile), F32),
            dma((5,)), dma((4, 8)), dma((4, 8)), dma((2, 8)), dma((2, 8)), pltpu.SemaphoreType.REGULAR((3,)),
            dma((8,)), dma((8,)), dma((16,)), dma((16,)), dma((8,)), dma((8,)),
            dma((16,)), dma((16,)), dma((8,)), dma((8,)), dma((16,)), dma((16,)),
        ],
        compiler_params=pltpu.CompilerParams(
            collective_id=0, has_side_effects=True, vmem_limit_bytes=48 << 20
        ),
        name="unet_levels",
    )(
        *(
            pltpu.with_memory_space_constraint(value, pltpu.HBM)
            for value in (
                volume.reshape(fine), fine_cotangent.reshape(fine),
                coarse_cotangent.reshape(coarse), kf, kc,
            )
        )
    )
    fo, co, vg, fk, ck = pl.pallas_call(
        emit_kernel,
        out_shape=[
            jax.ShapeDtypeStruct(fine, BF16),
            jax.ShapeDtypeStruct(coarse, BF16),
            jax.ShapeDtypeStruct(fine, BF16),
            jax.ShapeDtypeStruct((27, C1, C1), F32),
            jax.ShapeDtypeStruct((27, C1, C2), F32),
        ],
        in_specs=[vmem] * 5,
        out_specs=[hbm] * 5,
        scratch_shapes=[V((27, C1, C1), F32), V((27, C1, C2), F32), dma((5,))],
        compiler_params=pltpu.CompilerParams(vmem_limit_bytes=8 << 20),
        name="emit",
    )(*parts)
    return (
        fo.reshape(volume.shape),
        co.reshape(coarse_cotangent.shape),
        vg.reshape(volume.shape),
        fk.reshape(fine_kernel.shape),
        ck.reshape(3, 3, 3, C1, C2).transpose(0, 1, 2, 4, 3),
    )


def solution(mesh):
    block = P(None, "gx", "gy", None)
    return jax.shard_map(
        local,
        mesh=mesh,
        in_specs=(block, P(), P(), block, block),
        out_specs=(block, block, block, P(), P()),
        check_vma=False,
    )
```

```python
import jax
import jax.numpy as jnp
from jax import lax
from jax.experimental import pallas as pl
from jax.experimental.pallas import tpu as pltpu
from jax.sharding import PartitionSpec as P

F32 = jnp.float32
BF16 = jnp.bfloat16
MESH = pl.DeviceIdType.MESH
C1, C2 = 16, 32
D, R, W = 4, 8, 256
HD, HR, HW = 2, 4, 128
NGX, NGY = 32, 4
DIRS = [(-1, -1), (-1, 1), (1, -1), (1, 1), (-1, 0), (1, 0), (0, -1), (0, 1)]
NT = (((1,), (1,)), ((), ()))


def dot(a, b):
    return jnp.dot(a, b, preferred_element_type=F32)


def dot_nt(a, b):
    return lax.dot_general(a, b, NT, preferred_element_type=F32)


def shifted(x):
    n = x.shape[1]
    lane = lax.broadcasted_iota(jnp.int32, x.shape, 1)
    before = jnp.where(lane == 0, 0.0, pltpu.roll(x, 1, axis=1))
    after = jnp.where(lane == n - 1, 0.0, pltpu.roll(x, n - 1, axis=1))
    return before.astype(BF16), after.astype(BF16)


def exists(gx, gy, sx, sy):
    cond = None
    for ok in (
        [gx < NGX - 1] if sx == 1 else [gx > 0] if sx == -1 else []
    ) + ([gy < NGY - 1] if sy == 1 else [gy > 0] if sy == -1 else []):
        cond = ok if cond is None else jnp.logical_and(cond, ok)
    return cond


def span(s, h, n, sending):
    if s == 0:
        return h, n
    if sending:
        return (n, h) if s == 1 else (h, h)
    return (0, h) if s == 1 else (h + n, h)


class Halo:
    def __init__(self, buf, chan, h, nz, ny, send_sem, recv_sem, gx, gy):
        self.buf, self.chan, self.h, self.nz, self.ny = buf, chan, h, nz, ny
        self.send_sem, self.recv_sem, self.gx, self.gy = send_sem, recv_sem, gx, gy

    def part(self, sx, sy, sending):
        z0, zn = span(sx, self.h, self.nz, sending)
        y0, yn = span(sy, self.h, self.ny, sending)
        return self.buf.at[pl.ds(z0, zn), pl.ds(y0, yn), self.chan, :]

    def desc(self, i):
        sx, sy = DIRS[i]
        return pltpu.make_async_remote_copy(
            src_ref=self.part(sx, sy, True),
            dst_ref=self.part(sx, sy, False),
            send_sem=self.send_sem.at[i],
            recv_sem=self.recv_sem.at[i],
            device_id=(self.gx + sx, self.gy + sy),
            device_id_type=MESH,
        )

    def clear_edges(self):
        h, nz, ny = self.h, self.nz, self.ny
        for s, n, axis, g, last in (
            (-1, nz, 0, self.gx, 0),
            (1, nz, 0, self.gx, NGX - 1),
            (-1, ny, 1, self.gy, 0),
            (1, ny, 1, self.gy, NGY - 1),
        ):
            at = 0 if s == -1 else h + n
            rows = pl.ds(at, h)

            @pl.when(g == last)
            def _(axis=axis, rows=rows):
                index = (rows, slice(None)) if axis == 0 else (slice(None), rows)
                view = self.buf.at[(*index, self.chan, slice(None))]
                view[...] = jnp.zeros(view.shape, view.dtype)

    def start(self):
        for i, (sx, sy) in enumerate(DIRS):

            @pl.when(exists(self.gx, self.gy, sx, sy))
            def _(i=i):
                self.desc(i).start()

    def wait_recv(self, chosen=range(8)):
        for i in chosen:
            sx, sy = DIRS[i]

            @pl.when(exists(self.gx, self.gy, -sx, -sy))
            def _(i=i):
                self.desc(i).wait_recv()

    def wait_send(self):
        for i, (sx, sy) in enumerate(DIRS):

            @pl.when(exists(self.gx, self.gy, sx, sy))
            def _(i=i):
                self.desc(i).wait_send()


class PlaneHalo(Halo):
    def plane(self, p, i):
        sx, sy = DIRS[i]
        y0, yn = span(sy, self.h, self.ny, True)
        y1, _ = span(sy, self.h, self.ny, False)
        return pltpu.make_async_remote_copy(
            src_ref=self.buf.at[pl.ds(p + self.h, 1), pl.ds(y0, yn), self.chan, :],
            dst_ref=self.buf.at[pl.ds(p + self.h - 2 * sx, 1), pl.ds(y1, yn), self.chan, :],
            send_sem=self.send_sem.at[p, i],
            recv_sem=self.recv_sem.at[p, i],
            device_id=(self.gx + sx, self.gy + sy),
            device_id_type=MESH,
        )

    def start(self, p):
        for i, (sx, sy) in enumerate(DIRS):

            @pl.when(exists(self.gx, self.gy, sx, sy))
            def _(i=i):
                self.plane(p, i).start()

    def wait_recv(self, chosen):
        for i in chosen:
            sx, sy = DIRS[i]

            @pl.when(exists(self.gx, self.gy, -sx, -sy))
            def _(i=i):
                for p in range(2):
                    self.plane(p, i).wait_recv()

    def wait_send(self):
        for i, (sx, sy) in enumerate(DIRS):

            @pl.when(exists(self.gx, self.gy, sx, sy))
            def _(i=i):
                for p in range(2):
                    self.plane(p, i).wait_send()


class AllReduce:
    def __init__(self, terms, rs, bx, fin, sems, na, nb, a, b, dev_a, dev_b):
        self.terms, self.rs, self.bx, self.fin = terms, rs, bx, fin
        self.na, self.nb, self.a, self.b = na, nb, a, b
        self.dev_a, self.dev_b = dev_a, dev_b
        self.rs_s, self.rs_r, self.b_s, self.b_r, self.g_s, self.g_r = sems

    def rs_copy(self, k):
        d = lax.rem(self.a + k, self.na)
        return pltpu.make_async_remote_copy(
            self.terms.at[d], self.rs.at[k], self.rs_s.at[k], self.rs_r.at[k], self.dev_a(d), MESH
        )

    def b_copy(self, k):
        d = lax.rem(self.b + k, self.nb)
        return pltpu.make_async_remote_copy(
            self.bx.at[self.b], self.bx.at[self.b], self.b_s.at[k], self.b_r.at[k], self.dev_b(d), MESH
        )

    def g_copy(self, k):
        d = lax.rem(self.a + k, self.na)
        return pltpu.make_async_remote_copy(
            self.fin.at[self.a], self.fin.at[self.a], self.g_s.at[k], self.g_r.at[k], self.dev_a(d), MESH
        )

    def start_scatter(self):
        for k in range(1, self.na):
            self.rs_copy(k).start()

    def start_exchange(self):
        total = self.terms[self.a]
        for k in range(1, self.na):
            self.rs_copy(k).wait_recv()
        for k in range(1, self.na):
            total = total + self.rs[k]
        self.bx[self.b] = total
        for k in range(1, self.nb):
            self.b_copy(k).start()

    def start_gather(self):
        for k in range(1, self.nb):
            self.b_copy(k).wait_recv()
        total = self.bx[0]
        for k in range(1, self.nb):
            total = total + self.bx[k]
        self.fin[self.a] = total
        for k in range(1, self.na):
            self.g_copy(k).start()

    def finish(self):
        for k in range(1, self.na):
            self.g_copy(k).wait_recv()

    def wait_send(self):
        for k in range(1, self.na):
            self.rs_copy(k).wait_send()
            self.g_copy(k).wait_send()
        for k in range(1, self.nb):
            self.b_copy(k).wait_send()


def kernel(
    vol_hbm, fcot_hbm, ccot_hbm, kf_hbm, kc_hbm,
    fo_ref, co_ref, vg_ref, ffin, cfin,
    raw_v, raw_f, raw_c, kf, kc, st_v, st_f, st_c, st_o, st_co,
    vp, cp, qp, tp, sp, fob, g1, fg, csb, cob, w32, wc32, w32t, wc32n, packed,
    wide_f, wide_t, wide_s, wide_c, band_f, band_t, band_s, band_c, ft, ct,
    frs, fbx, crs, cbx,
    in_sem, hs, hr, qs, qr, know, f_rs_s, f_rs_r, f_b_s, f_b_r, f_g_s, f_g_r,
    c_rs_s, c_rs_r, c_b_s, c_b_r, c_g_s, c_g_r,
):
    gx, gy = lax.axis_index("gx"), lax.axis_index("gy")
    mid = pl.ds(C1, C1)
    barrier = pltpu.get_barrier_semaphore()
    n_halo = 0
    for sx, sy in DIRS:
        near = exists(gx, gy, sx, sy)
        n_halo = n_halo + near.astype(jnp.int32)

        @pl.when(near)
        def _(sx=sx, sy=sy):
            pl.semaphore_signal(
                barrier, inc=1, device_id=(gx + sx, gy + sy), device_id_type=MESH
            )

    zi, hi = lax.rem(gx, 4), lax.div(gx, 4)
    ring = [lax.div(hi, 4) * 16 + lax.rem(hi + k, 4) * 4 + zi for k in (1, 3)]
    across = lax.rem(gx + 16, NGX)
    for far in (*ring, across):
        pl.semaphore_signal(barrier, inc=1, device_id=(far, gy), device_id_type=MESH)

    def tell(one, device):
        pl.semaphore_signal(know.at[one], inc=1, device_id=(device, gy), device_id_type=MESH)

    loads = [
        pltpu.make_async_copy(src, dst, in_sem.at[i])
        for i, (src, dst) in enumerate(
            (
                (vol_hbm, raw_v), (kf_hbm, kf), (kc_hbm, kc),
                (ccot_hbm, raw_c), (fcot_hbm, raw_f),
            )
        )
    ]
    for load in loads:
        load.start()

    y_lo, core = lax.div(gy, 2), lax.rem(gy, 2)
    base = hi * 4

    def c_dev_a(d):
        return (base + lax.div(d, 4), lax.rem(d, 4))

    def c_dev_b(d):
        return (d * 4 + zi, gy)

    def f_dev_a(d):
        return (base + lax.div(d, 2), y_lo * 2 + lax.rem(d, 2))

    def f_dev_b(d):
        return (lax.div(d, 2) * 4 + zi, lax.rem(d, 2) * 2 + core)

    a_c, a_f, b_f = zi * 4 + gy, zi * 2 + core, hi * 2 + y_lo

    def hear_ring():
        for one in range(2):
            pl.semaphore_wait(know.at[one], 1)
        tell(2, across)

    def hear_across():
        pl.semaphore_wait(know.at[2], 1)

    vhalo = Halo(vp, mid, 1, D, R, hs.at[0], hr.at[0], gx, gy)
    chalo = Halo(cp, slice(None), 1, HD, HR, hs.at[1], hr.at[1], gx, gy)
    qhalo = PlaneHalo(qp, mid, 2, HD, HR, qs, qr, gx, gy)
    shalo = Halo(sp, mid, 1, D, R, hs.at[3], hr.at[3], gx, gy)
    f_sum = AllReduce(
        ft, frs, fbx, ffin, (f_rs_s, f_rs_r, f_b_s, f_b_r, f_g_s, f_g_r),
        8, 16, a_f, b_f, f_dev_a, f_dev_b,
    )
    c_sum = AllReduce(
        ct, crs, cbx, cfin, (c_rs_s, c_rs_r, c_b_s, c_b_r, c_g_s, c_g_r),
        16, 8, a_c, hi, c_dev_a, c_dev_b,
    )
    for halo in (vhalo, chalo, qhalo, shalo):
        halo.clear_edges()

    loads[0].wait()
    for t in range(2):
        st_v[t] = raw_v[:, t * 128 : (t + 1) * 128].astype(F32)
    for z in range(D):
        for y in range(R):
            for t in range(2):
                vp[z + 1, y + 1, mid, pl.ds(t * 128, 128)] = st_v[
                    t, pl.ds(z * R + y, C1, stride=D * R), :
                ].astype(BF16)
    pl.semaphore_wait(barrier, n_halo + 3)
    vhalo.start()
    for one in range(2):
        tell(one, ring[one])

    def put_shifts(buf, z, y, order):
        before, after = shifted(buf[z, y, mid, :].astype(F32))
        low, high = (before, after) if order > 0 else (after, before)
        buf[z, y, pl.ds(0, C1), :] = low
        buf[z, y, pl.ds(2 * C1, C1), :] = high

    def own_shifts(buf, h, nz, ny, order):
        @pl.loop(0, nz)
        def _(z):
            for y in range(ny):
                put_shifts(buf, z + h, y + h, order)

    def halo_shifts(buf, h, nz, ny, order):
        @pl.loop(0, h)
        def _(z):
            for y in range(ny + 2 * h):
                put_shifts(buf, z, y, order)
                put_shifts(buf, z + h + nz, y, order)

        @pl.loop(0, nz)
        def _(z):
            for y in range(h):
                put_shifts(buf, z + h, y, order)
                put_shifts(buf, z + h, y + h + ny, order)

    def taps(buf, z, y, back=False):
        rows = []
        for a in range(3):
            for b in range(3):
                da, db = (2 - a, 2 - b) if back else (a, b)
                rows.append(buf[z + da, y + db])
        return jnp.concatenate(rows, axis=0)

    own_shifts(vp, 1, D, R, 1)
    for one in (1, 2):
        loads[one].wait()
    for tap in range(27):
        w32[:, tap * C1 : (tap + 1) * C1] = kf[tap * C1 : (tap + 1) * C1, :].astype(F32)
        wc32[:, tap * C2 : (tap + 1) * C2] = kc[tap * C1 : (tap + 1) * C1, :].astype(F32)

    def eye(n):
        rows = lax.broadcasted_iota(jnp.int32, (n, n), 0)
        return (rows == lax.broadcasted_iota(jnp.int32, (n, n), 1)).astype(F32).astype(BF16)

    wf = w32[...].astype(BF16)
    w32t[...] = dot_nt(eye(C1), kf[...])
    wc32n[...] = dot_nt(eye(C2), kc[...])
    for band in (wide_f, wide_t, wide_s, wide_c):
        band[...] = jnp.zeros(band.shape, F32)
    for a in range(3):
        for r in range(4):
            rows = pl.ds(r * C1, C1)
            wide_f[rows, pl.ds(a * 288 + r * 48, 144)] = w32[:, a * 144 : (a + 1) * 144]
            for b in range(3):
                at = a * 3 + b
                wide_t[rows, pl.ds(a * 288 + (r + 2 - b) * 48, 48)] = w32t[
                    :, at * 48 : (at + 1) * 48
                ]
                wide_s[rows, pl.ds(a * 576 + (r + 2 - b) * 96, 96)] = wc32[
                    :, at * 96 : (at + 1) * 96
                ]
        for r in range(2):
            wide_c[pl.ds(r * C2, C2), pl.ds(a * 192 + r * 48, 144)] = wc32n[
                :, a * 144 : (a + 1) * 144
            ]
    band_f[...] = wide_f[...].astype(BF16)
    band_t[...] = wide_t[...].astype(BF16)
    band_s[...] = wide_s[...].astype(BF16)
    band_c[...] = wide_c[...].astype(BF16)
    packed[...] = jnp.zeros(packed.shape, F32)
    loads[3].wait()
    st_c[...] = raw_c[...].astype(F32)
    for z in range(HD):
        for y in range(HR):
            cp[z + 1, y + 1] = st_c[pl.ds(z * HR + y, C2, stride=HD * HR), :].astype(BF16)
    chalo.start()

    def block(buf, z, y, n):
        return buf[z, pl.ds(y, n)].reshape(n * buf.shape[2], buf.shape[3])

    def fine_band(z, y0):
        four = dot(
            band_f[...], jnp.concatenate([block(vp, z + a, y0, 6) for a in range(3)], axis=0)
        )
        for r in range(4):
            fine_cell(z, y0 + r, four[r * C1 : (r + 1) * C1])

    def fine_row(z, y):
        fine_cell(z, y, dot(wf, taps(vp, z, y)))

    def fine_cell(z, y, pre):
        s = jax.nn.sigmoid(pre)
        out = (vp[z + 1, y + 1, mid, :].astype(F32) + pre * s).astype(BF16)
        g1[z, y] = s * (1.0 + pre * (1.0 - s))
        fob[z, y] = out

    @pl.loop(1, D - 1)
    def _(z):
        for y in range(1, R - 1):
            fine_row(z, y)

    pool_row = lax.broadcasted_iota(jnp.int32, (W, HW), 0)
    pool_col = lax.broadcasted_iota(jnp.int32, (W, HW), 1)
    pool_mat = (lax.div(pool_row, 2) == pool_col).astype(F32).astype(BF16)
    up_row = lax.broadcasted_iota(jnp.int32, (HW, 3 * W), 0)
    up_col = lax.broadcasted_iota(jnp.int32, (HW, 3 * W), 1)
    up_mat = (
        up_row == lax.div(lax.rem(up_col, W), 2) + 1 - lax.div(up_col, W)
    ).astype(F32).astype(BF16)
    loads[4].wait()
    for t in range(2):
        st_f[t] = raw_f[:, t * 128 : (t + 1) * 128].astype(F32)
    vhalo.wait_recv((6, 7))

    @pl.loop(0, D)
    def _(z):
        for y in (0, R + 1):
            put_shifts(vp, z + 1, y, 1)

    late = (zi == 0).astype(jnp.int32)
    for side in (late, 1 - late):

        @pl.when(side == 0)
        def _():
            vhalo.wait_recv((2, 3, 5))

        @pl.when(side == 1)
        def _():
            vhalo.wait_recv((0, 1, 4))

        for y in range(R + 2):
            put_shifts(vp, side * (D + 1), y, 1)
        for y in (0, 4):
            fine_band(side * (D - 1), y)
        for y in (0, R - 1):
            fine_row(side + 1, y)
        for yc in range(HR):
            four = fob[pl.ds(side * 2, 2), pl.ds(yc * 2, 2)].reshape(4 * C1, W)
            half = dot(four, pool_mat)
            total = half[0:16] + half[16:32] + half[32:48] + half[48:64]
            qp[side + 2, yc + 2, mid, :] = (total * 0.125).astype(BF16)
        qhalo.start(side)

    hear_ring()
    own_shifts(qp, 2, HD, HR, 1)

    def rows_out(rows, store):
        @pl.loop(0, D)
        def _(z):
            for y in range(R):
                value = rows[z, y].astype(F32)
                for t in range(2):
                    store[t, pl.ds(z * R + y, C1, stride=D * R), :] = value[
                        :, t * 128 : (t + 1) * 128
                    ]

    rows_out(fob, st_o)
    for t in range(2):
        fo_ref[:, t * 128 : (t + 1) * 128] = st_o[t].astype(BF16)
    chalo.wait_recv()
    qhalo.wait_recv((6, 7))

    @pl.loop(0, HD)
    def _(z):
        for y in (0, 1, HR + 2, HR + 3):
            put_shifts(qp, z + 2, y, 1)

    for zp in (late, 1 - late):

        @pl.when(zp == 0)
        def _():
            qhalo.wait_recv((2, 3, 5))

        @pl.when(zp == 1)
        def _():
            qhalo.wait_recv((0, 1, 4))

        for k in range(2):
            for y in range(HR + 4):
                put_shifts(qp, zp * 4 + k, y, 1)
        for y0 in range(0, HR + 2, 2):
            two = [
                jnp.concatenate([block(qp, zp * 2 + k + a, y0, 4) for a in range(3)], axis=0)
                for k in range(2)
            ]
            pair = dot(band_c[...], jnp.concatenate(two, axis=1))
            for r in range(2):
                for k in range(2):
                    z, y = zp * 2 + k, y0 + r
                    pre = pair[r * C2 : (r + 1) * C2, k * HW : (k + 1) * HW]
                    s = jax.nn.sigmoid(pre)
                    slope = cp[z, y].astype(F32) * (s * (1.0 + pre * (1.0 - s)))
                    csb[z, y] = slope.astype(BF16)
                    if 1 <= y <= HR:
                        cob[z, y - 1] = (pre * s).astype(BF16)
        for k in range(2):
            z = zp * 2 + k
            wide = dot(csb[z].reshape((HR + 2) * C2, HW), up_mat).astype(BF16)
            for c in range(3):
                tp[z, :, pl.ds(c * C2, C2), :] = wide[:, c * W : (c + 1) * W].reshape(
                    HR + 2, C2, W
                )

    hear_across()

    def turned(rows):
        rows = jnp.concatenate([rows, jnp.zeros((80, rows.shape[1]), F32)], axis=0)
        return jnp.transpose(rows)

    cells = [(z + 1, y + 1) for z in range(HD) for y in range(HR)]
    ck = dot_nt(
        jnp.concatenate([taps(qp, *at) for at in cells], axis=1),
        jnp.concatenate([csb[at] for at in cells], axis=1),
    )
    ck = turned(ck)
    for i in range(4):
        for t in range(4):
            ct[i * 4 + t] = ck[i * 8 : (i + 1) * 8, t * 128 : (t + 1) * 128]
    c_sum.start_scatter()

    @pl.loop(0, HD)
    def _(zc):
        four = dot(
            band_s[...], jnp.concatenate([block(tp, zc + 2 - a, 0, 6) for a in range(3)], axis=0)
        )
        for yc in range(HR):
            spread = four[yc * C1 : (yc + 1) * C1] * 0.125
            for zz in range(2):
                for yy in range(2):
                    z, y = zc * 2 + zz, yc * 2 + yy
                    cot = jnp.concatenate(
                        [st_f[t, pl.ds(z * R + y, C1, stride=D * R), :] for t in range(2)], axis=1
                    )
                    grad = cot + spread
                    fg[z, y] = grad
                    sp[z + 1, y + 1, mid, :] = (grad * g1[z, y]).astype(BF16)

    shalo.start()

    def slope_rows(z, yb):
        if not 0 <= z < D:
            return jnp.zeros((4 * C1, W), BF16)
        return sp[z + 1, pl.ds(yb * 4 + 1, 4), mid, :].reshape(4 * C1, W)

    steps = [(z, yb) for z in range(D + 2) for yb in range(2)]
    pairs = dot_nt(
        jnp.concatenate([block(vp, z, yb * 4, 6) for z, yb in steps], axis=1),
        jnp.concatenate(
            [
                jnp.concatenate([slope_rows(z - a, yb) for a in range(3)], axis=0)
                for z, yb in steps
            ],
            axis=1,
        ),
    )
    pairs = jnp.concatenate([pairs, jnp.zeros((288, 64), F32)], axis=1)
    pairs = jnp.transpose(jnp.concatenate([pairs, jnp.zeros((96, 256), F32)], axis=0))
    for a in range(3):
        total = pairs[a * 64 : a * 64 + 16, 0:144]
        for y in range(1, 4):
            total = total + pairs[a * 64 + y * 16 : a * 64 + y * 16 + 16, y * 48 : y * 48 + 144]
        packed[:, a * 144 : (a + 1) * 144] = total
    fk = packed[...]
    for i in range(2):
        for t in range(4):
            ft[i * 4 + t] = fk[i * 8 : (i + 1) * 8, t * 128 : (t + 1) * 128]
    f_sum.start_scatter()
    c_sum.start_exchange()
    own_shifts(sp, 1, D, R, -1)
    f_sum.start_exchange()
    shalo.wait_recv()
    halo_shifts(sp, 1, D, R, -1)

    @pl.loop(0, D)
    def _(z):
        for y0 in (0, 4):
            four = dot(
                band_t[...],
                jnp.concatenate([block(sp, z + 2 - a, y0, 6) for a in range(3)], axis=0),
            )
            for r in range(4):
                fg[z, y0 + r] = fg[z, y0 + r] + four[r * C1 : (r + 1) * C1]

    c_sum.start_gather()
    f_sum.start_gather()
    rows_out(fg, st_o)
    for t in range(2):
        vg_ref[:, t * 128 : (t + 1) * 128] = st_o[t].astype(BF16)
    for z in range(HD):
        for y in range(HR):
            st_co[pl.ds(z * HR + y, C2, stride=HD * HR), :] = cob[z + 1, y].astype(F32)
    co_ref[...] = st_co[...].astype(BF16)
    for one in (vhalo, chalo, qhalo, shalo, c_sum, f_sum):
        one.wait_send()
    c_sum.finish()
    f_sum.finish()


def emit_kernel(fo, co, vg, ffin, cfin, fo_hbm, co_hbm, vg_hbm, fk_hbm, ck_hbm, fk, ck, sem):
    copies = [
        pltpu.make_async_copy(src, dst, sem.at[i])
        for i, (src, dst) in enumerate(
            ((fo, fo_hbm), (vg, vg_hbm), (co, co_hbm), (fk, fk_hbm), (ck, ck_hbm))
        )
    ]
    for i in range(3):
        copies[i].start()
    for i in range(2):
        for t in range(4):
            tile = ffin[i * 4 + t] * (1048576.0**-0.5)
            for k in range(8):
                tap = t * 8 + k
                if tap < 27:
                    fk[tap, pl.ds(i * 8, 8), :] = tile[:, k * C1 : (k + 1) * C1]
    copies[3].start()
    for t in range(4):
        rows = jnp.concatenate([cfin[i * 4 + t] for i in range(4)], axis=0)
        cols = jnp.transpose(rows * (131072.0**-0.5))
        for k in range(8):
            tap = t * 8 + k
            if tap < 27:
                ck[tap] = cols[k * C1 : (k + 1) * C1, :]
    copies[4].start()
    for one in copies:
        one.wait()


def local(volume, fine_kernel, coarse_kernel, fine_cotangent, coarse_cotangent):
    kf = fine_kernel.reshape(27 * C1, C1)
    kc = coarse_kernel.transpose(0, 1, 2, 4, 3).reshape(27 * C1, C2)
    hbm = pl.BlockSpec(memory_space=pltpu.HBM)
    vmem = pl.BlockSpec(memory_space=pltpu.VMEM)
    dma = pltpu.SemaphoreType.DMA
    V = pltpu.VMEM
    tile = (8, 128)
    fine, coarse = (C1 * D * R, W), (C2 * HD * HR, HW)
    parts = pl.pallas_call(
        kernel,
        out_shape=[
            jax.ShapeDtypeStruct(fine, BF16),
            jax.ShapeDtypeStruct(coarse, BF16),
            jax.ShapeDtypeStruct(fine, BF16),
            jax.ShapeDtypeStruct((8, *tile), F32),
            jax.ShapeDtypeStruct((16, *tile), F32),
        ],
        in_specs=[hbm] * 5,
        out_specs=[vmem] * 5,
        scratch_shapes=[
            V(fine, BF16), V(fine, BF16), V(coarse, BF16),
            V((27 * C1, C1), BF16), V((27 * C1, C2), BF16),
            V((2, C1 * D * R, 128), F32), V((2, C1 * D * R, 128), F32), V(coarse, F32),
            V((2, C1 * D * R, 128), F32), V(coarse, F32),
            V((D + 2, R + 2, 3 * C1, W), BF16),
            V((HD + 2, HR + 2, C2, HW), BF16),
            V((HD + 4, HR + 4, 3 * C1, HW), BF16),
            V((HD + 2, HR + 2, 3 * C2, W), BF16),
            V((D + 2, R + 2, 3 * C1, W), BF16),
            V((D, R, C1, W), BF16), V((D, R, C1, W), F32), V((D, R, C1, W), F32),
            V((HD + 2, HR + 2, C2, HW), BF16), V((HD + 2, HR, C2, HW), BF16),
            V((C1, 27 * C1), F32), V((C1, 27 * C2), F32),
            V((C1, 27 * C1), F32), V((C2, 27 * C1), F32), V((C1, 512), F32),
            V((64, 864), F32), V((64, 864), F32), V((64, 1728), F32), V((64, 576), F32),
            V((64, 864), BF16), V((64, 864), BF16), V((64, 1728), BF16), V((64, 576), BF16),
            V((8, *tile), F32), V((16, *tile), F32),
            V((8, *tile), F32), V((16, *tile), F32),
            V((16, *tile), F32), V((8, *tile), F32),
            dma((5,)), dma((4, 8)), dma((4, 8)), dma((2, 8)), dma((2, 8)), pltpu.SemaphoreType.REGULAR((3,)),
            dma((8,)), dma((8,)), dma((16,)), dma((16,)), dma((8,)), dma((8,)),
            dma((16,)), dma((16,)), dma((8,)), dma((8,)), dma((16,)), dma((16,)),
        ],
        compiler_params=pltpu.CompilerParams(
            collective_id=0, has_side_effects=True, vmem_limit_bytes=48 << 20
        ),
        name="unet_levels",
    )(
        *(
            pltpu.with_memory_space_constraint(value, pltpu.HBM)
            for value in (
                volume.reshape(fine), fine_cotangent.reshape(fine),
                coarse_cotangent.reshape(coarse), kf, kc,
            )
        )
    )
    fo, co, vg, fk, ck = pl.pallas_call(
        emit_kernel,
        out_shape=[
            jax.ShapeDtypeStruct(fine, BF16),
            jax.ShapeDtypeStruct(coarse, BF16),
            jax.ShapeDtypeStruct(fine, BF16),
            jax.ShapeDtypeStruct((27, C1, C1), F32),
            jax.ShapeDtypeStruct((27, C1, C2), F32),
        ],
        in_specs=[vmem] * 5,
        out_specs=[hbm] * 5,
        scratch_shapes=[V((27, C1, C1), F32), V((27, C1, C2), F32), dma((5,))],
        compiler_params=pltpu.CompilerParams(vmem_limit_bytes=8 << 20),
        name="emit",
    )(*parts)
    return (
        fo.reshape(volume.shape),
        co.reshape(coarse_cotangent.shape),
        vg.reshape(volume.shape),
        fk.reshape(fine_kernel.shape),
        ck.reshape(3, 3, 3, C1, C2).transpose(0, 1, 2, 4, 3),
    )


def solution(mesh):
    block = P(None, "gx", "gy", None)
    return jax.shard_map(
        local,
        mesh=mesh,
        in_specs=(block, P(), P(), block, block),
        out_specs=(block, block, block, P(), P()),
        check_vma=False,
    )
```

```python
import jax
import jax.numpy as jnp
from jax import lax
from jax.experimental import pallas as pl
from jax.experimental.pallas import tpu as pltpu
from jax.sharding import PartitionSpec as P

F32 = jnp.float32
BF16 = jnp.bfloat16
MESH = pl.DeviceIdType.MESH
C1, C2 = 16, 32
D, R, W = 4, 8, 256
HD, HR, HW = 2, 4, 128
NGX, NGY = 32, 4
DIRS = [(-1, -1), (-1, 1), (1, -1), (1, 1), (-1, 0), (1, 0), (0, -1), (0, 1)]
NT = (((1,), (1,)), ((), ()))


def dot(a, b):
    return jnp.dot(a, b, preferred_element_type=F32)


def dot_nt(a, b):
    return lax.dot_general(a, b, NT, preferred_element_type=F32)


def shifted(x):
    n = x.shape[1]
    lane = lax.broadcasted_iota(jnp.int32, x.shape, 1)
    before = jnp.where(lane == 0, 0.0, pltpu.roll(x, 1, axis=1))
    after = jnp.where(lane == n - 1, 0.0, pltpu.roll(x, n - 1, axis=1))
    return before.astype(BF16), after.astype(BF16)


def exists(gx, gy, sx, sy):
    cond = None
    for ok in (
        [gx < NGX - 1] if sx == 1 else [gx > 0] if sx == -1 else []
    ) + ([gy < NGY - 1] if sy == 1 else [gy > 0] if sy == -1 else []):
        cond = ok if cond is None else jnp.logical_and(cond, ok)
    return cond


def span(s, h, n, sending):
    if s == 0:
        return h, n
    if sending:
        return (n, h) if s == 1 else (h, h)
    return (0, h) if s == 1 else (h + n, h)


class Halo:
    def __init__(self, buf, chan, h, nz, ny, send_sem, recv_sem, gx, gy):
        self.buf, self.chan, self.h, self.nz, self.ny = buf, chan, h, nz, ny
        self.send_sem, self.recv_sem, self.gx, self.gy = send_sem, recv_sem, gx, gy

    def part(self, sx, sy, sending):
        z0, zn = span(sx, self.h, self.nz, sending)
        y0, yn = span(sy, self.h, self.ny, sending)
        return self.buf.at[pl.ds(z0, zn), pl.ds(y0, yn), self.chan, :]

    def desc(self, i):
        sx, sy = DIRS[i]
        return pltpu.make_async_remote_copy(
            src_ref=self.part(sx, sy, True),
            dst_ref=self.part(sx, sy, False),
            send_sem=self.send_sem.at[i],
            recv_sem=self.recv_sem.at[i],
            device_id=(self.gx + sx, self.gy + sy),
            device_id_type=MESH,
        )

    def clear_edges(self):
        h, nz, ny = self.h, self.nz, self.ny
        for s, n, axis, g, last in (
            (-1, nz, 0, self.gx, 0),
            (1, nz, 0, self.gx, NGX - 1),
            (-1, ny, 1, self.gy, 0),
            (1, ny, 1, self.gy, NGY - 1),
        ):
            at = 0 if s == -1 else h + n
            rows = pl.ds(at, h)

            @pl.when(g == last)
            def _(axis=axis, rows=rows):
                index = (rows, slice(None)) if axis == 0 else (slice(None), rows)
                view = self.buf.at[(*index, self.chan, slice(None))]
                view[...] = jnp.zeros(view.shape, view.dtype)

    def start(self):
        for i, (sx, sy) in enumerate(DIRS):

            @pl.when(exists(self.gx, self.gy, sx, sy))
            def _(i=i):
                self.desc(i).start()

    def wait_recv(self, chosen=range(8)):
        for i in chosen:
            sx, sy = DIRS[i]

            @pl.when(exists(self.gx, self.gy, -sx, -sy))
            def _(i=i):
                self.desc(i).wait_recv()

    def wait_send(self):
        for i, (sx, sy) in enumerate(DIRS):

            @pl.when(exists(self.gx, self.gy, sx, sy))
            def _(i=i):
                self.desc(i).wait_send()


class PlaneHalo(Halo):
    def plane(self, p, i):
        sx, sy = DIRS[i]
        y0, yn = span(sy, self.h, self.ny, True)
        y1, _ = span(sy, self.h, self.ny, False)
        return pltpu.make_async_remote_copy(
            src_ref=self.buf.at[pl.ds(p + self.h, 1), pl.ds(y0, yn), self.chan, :],
            dst_ref=self.buf.at[pl.ds(p + self.h - 2 * sx, 1), pl.ds(y1, yn), self.chan, :],
            send_sem=self.send_sem.at[p, i],
            recv_sem=self.recv_sem.at[p, i],
            device_id=(self.gx + sx, self.gy + sy),
            device_id_type=MESH,
        )

    def start(self, p):
        for i, (sx, sy) in enumerate(DIRS):

            @pl.when(exists(self.gx, self.gy, sx, sy))
            def _(i=i):
                self.plane(p, i).start()

    def wait_recv(self, chosen):
        for i in chosen:
            sx, sy = DIRS[i]

            @pl.when(exists(self.gx, self.gy, -sx, -sy))
            def _(i=i):
                for p in range(2):
                    self.plane(p, i).wait_recv()

    def wait_send(self):
        for i, (sx, sy) in enumerate(DIRS):

            @pl.when(exists(self.gx, self.gy, sx, sy))
            def _(i=i):
                for p in range(2):
                    self.plane(p, i).wait_send()


class AllReduce:
    def __init__(self, terms, rs, bx, fin, sems, na, nb, a, b, dev_a, dev_b):
        self.terms, self.rs, self.bx, self.fin = terms, rs, bx, fin
        self.na, self.nb, self.a, self.b = na, nb, a, b
        self.dev_a, self.dev_b = dev_a, dev_b
        self.rs_s, self.rs_r, self.b_s, self.b_r, self.g_s, self.g_r = sems

    def rs_copy(self, k):
        d = lax.rem(self.a + k, self.na)
        return pltpu.make_async_remote_copy(
            self.terms.at[d], self.rs.at[k], self.rs_s.at[k], self.rs_r.at[k], self.dev_a(d), MESH
        )

    def b_copy(self, k):
        d = lax.rem(self.b + k, self.nb)
        return pltpu.make_async_remote_copy(
            self.bx.at[self.b], self.bx.at[self.b], self.b_s.at[k], self.b_r.at[k], self.dev_b(d), MESH
        )

    def g_copy(self, k):
        d = lax.rem(self.a + k, self.na)
        return pltpu.make_async_remote_copy(
            self.fin.at[self.a], self.fin.at[self.a], self.g_s.at[k], self.g_r.at[k], self.dev_a(d), MESH
        )

    def start_scatter(self):
        for k in range(1, self.na):
            self.rs_copy(k).start()

    def start_exchange(self):
        total = self.terms[self.a]
        for k in range(1, self.na):
            self.rs_copy(k).wait_recv()
        for k in range(1, self.na):
            total = total + self.rs[k]
        self.bx[self.b] = total
        for k in range(1, self.nb):
            self.b_copy(k).start()

    def start_gather(self):
        for k in range(1, self.nb):
            self.b_copy(k).wait_recv()
        total = self.bx[0]
        for k in range(1, self.nb):
            total = total + self.bx[k]
        self.fin[self.a] = total
        for k in range(1, self.na):
            self.g_copy(k).start()

    def finish(self):
        for k in range(1, self.na):
            self.g_copy(k).wait_recv()

    def wait_send(self):
        for k in range(1, self.na):
            self.rs_copy(k).wait_send()
            self.g_copy(k).wait_send()
        for k in range(1, self.nb):
            self.b_copy(k).wait_send()


def kernel(
    vol_hbm, fcot_hbm, ccot_hbm, kf_hbm, kc_hbm,
    fo_ref, co_ref, vg_ref, ffin, cfin,
    raw_v, raw_f, raw_c, kf, kc, st_v, st_f, st_c, st_o, st_co,
    vp, cp, qp, tp, sp, fob, g1, fg, csb, cob, w32, wc32, w32t, wc32n, packed,
    wide_f, wide_t, wide_s, wide_c, band_f, band_t, band_s, band_c, ft, ct,
    frs, fbx, crs, cbx,
    in_sem, hs, hr, qs, qr, know, f_rs_s, f_rs_r, f_b_s, f_b_r, f_g_s, f_g_r,
    c_rs_s, c_rs_r, c_b_s, c_b_r, c_g_s, c_g_r,
):
    gx, gy = lax.axis_index("gx"), lax.axis_index("gy")
    mid = pl.ds(C1, C1)
    barrier = pltpu.get_barrier_semaphore()
    n_halo = 0
    for sx, sy in DIRS:
        near = exists(gx, gy, sx, sy)
        n_halo = n_halo + near.astype(jnp.int32)

        @pl.when(near)
        def _(sx=sx, sy=sy):
            pl.semaphore_signal(
                barrier, inc=1, device_id=(gx + sx, gy + sy), device_id_type=MESH
            )

    zi, hi = lax.rem(gx, 4), lax.div(gx, 4)
    ring = [lax.div(hi, 4) * 16 + lax.rem(hi + k, 4) * 4 + zi for k in (1, 3)]
    across = lax.rem(gx + 16, NGX)
    for far in (*ring, across):
        pl.semaphore_signal(barrier, inc=1, device_id=(far, gy), device_id_type=MESH)

    def tell(one, device):
        pl.semaphore_signal(know.at[one], inc=1, device_id=(device, gy), device_id_type=MESH)

    loads = [
        pltpu.make_async_copy(src, dst, in_sem.at[i])
        for i, (src, dst) in enumerate(
            (
                (vol_hbm, raw_v), (kf_hbm, kf), (kc_hbm, kc),
                (ccot_hbm, raw_c), (fcot_hbm, raw_f),
            )
        )
    ]
    for load in loads:
        load.start()

    y_lo, core = lax.div(gy, 2), lax.rem(gy, 2)
    base = hi * 4

    def c_dev_a(d):
        return (base + lax.div(d, 4), lax.rem(d, 4))

    def c_dev_b(d):
        return (d * 4 + zi, gy)

    def f_dev_a(d):
        return (base + lax.div(d, 2), y_lo * 2 + lax.rem(d, 2))

    def f_dev_b(d):
        return (lax.div(d, 2) * 4 + zi, lax.rem(d, 2) * 2 + core)

    a_c, a_f, b_f = zi * 4 + gy, zi * 2 + core, hi * 2 + y_lo

    def hear_ring():
        for one in range(2):
            pl.semaphore_wait(know.at[one], 1)
        tell(2, across)

    def hear_across():
        pl.semaphore_wait(know.at[2], 1)

    vhalo = Halo(vp, mid, 1, D, R, hs.at[0], hr.at[0], gx, gy)
    chalo = Halo(cp, slice(None), 1, HD, HR, hs.at[1], hr.at[1], gx, gy)
    qhalo = PlaneHalo(qp, mid, 2, HD, HR, qs, qr, gx, gy)
    shalo = Halo(sp, mid, 1, D, R, hs.at[3], hr.at[3], gx, gy)
    f_sum = AllReduce(
        ft, frs, fbx, ffin, (f_rs_s, f_rs_r, f_b_s, f_b_r, f_g_s, f_g_r),
        8, 16, a_f, b_f, f_dev_a, f_dev_b,
    )
    c_sum = AllReduce(
        ct, crs, cbx, cfin, (c_rs_s, c_rs_r, c_b_s, c_b_r, c_g_s, c_g_r),
        16, 8, a_c, hi, c_dev_a, c_dev_b,
    )
    for halo in (vhalo, chalo, qhalo, shalo):
        halo.clear_edges()

    loads[0].wait()
    for t in range(2):
        st_v[t] = raw_v[:, t * 128 : (t + 1) * 128].astype(F32)
    for z in range(D):
        for y in range(R):
            for t in range(2):
                vp[z + 1, y + 1, mid, pl.ds(t * 128, 128)] = st_v[
                    t, pl.ds(z * R + y, C1, stride=D * R), :
                ].astype(BF16)
    pl.semaphore_wait(barrier, n_halo + 3)
    vhalo.start()
    for one in range(2):
        tell(one, ring[one])

    def put_shifts(buf, z, y, order):
        before, after = shifted(buf[z, y, mid, :].astype(F32))
        low, high = (before, after) if order > 0 else (after, before)
        buf[z, y, pl.ds(0, C1), :] = low
        buf[z, y, pl.ds(2 * C1, C1), :] = high

    def own_shifts(buf, h, nz, ny, order):
        @pl.loop(0, nz)
        def _(z):
            for y in range(ny):
                put_shifts(buf, z + h, y + h, order)

    def halo_shifts(buf, h, nz, ny, order):
        @pl.loop(0, h)
        def _(z):
            for y in range(ny + 2 * h):
                put_shifts(buf, z, y, order)
                put_shifts(buf, z + h + nz, y, order)

        @pl.loop(0, nz)
        def _(z):
            for y in range(h):
                put_shifts(buf, z + h, y, order)
                put_shifts(buf, z + h, y + h + ny, order)

    def taps(buf, z, y, back=False):
        rows = []
        for a in range(3):
            for b in range(3):
                da, db = (2 - a, 2 - b) if back else (a, b)
                rows.append(buf[z + da, y + db])
        return jnp.concatenate(rows, axis=0)

    own_shifts(vp, 1, D, R, 1)
    for one in (1, 2):
        loads[one].wait()
    for tap in range(27):
        w32[:, tap * C1 : (tap + 1) * C1] = kf[tap * C1 : (tap + 1) * C1, :].astype(F32)
        wc32[:, tap * C2 : (tap + 1) * C2] = kc[tap * C1 : (tap + 1) * C1, :].astype(F32)

    def eye(n):
        rows = lax.broadcasted_iota(jnp.int32, (n, n), 0)
        return (rows == lax.broadcasted_iota(jnp.int32, (n, n), 1)).astype(F32).astype(BF16)

    wf = w32[...].astype(BF16)
    w32t[...] = dot_nt(eye(C1), kf[...])
    wc32n[...] = dot_nt(eye(C2), kc[...])
    for band in (wide_f, wide_t, wide_s, wide_c):
        band[...] = jnp.zeros(band.shape, F32)
    for a in range(3):
        for r in range(4):
            rows = pl.ds(r * C1, C1)
            wide_f[rows, pl.ds(a * 288 + r * 48, 144)] = w32[:, a * 144 : (a + 1) * 144]
            for b in range(3):
                at = a * 3 + b
                wide_t[rows, pl.ds(a * 288 + (r + 2 - b) * 48, 48)] = w32t[
                    :, at * 48 : (at + 1) * 48
                ]
                wide_s[rows, pl.ds(a * 576 + (r + 2 - b) * 96, 96)] = wc32[
                    :, at * 96 : (at + 1) * 96
                ]
        for r in range(2):
            wide_c[pl.ds(r * C2, C2), pl.ds(a * 192 + r * 48, 144)] = wc32n[
                :, a * 144 : (a + 1) * 144
            ]
    band_f[...] = wide_f[...].astype(BF16)
    band_t[...] = wide_t[...].astype(BF16)
    band_s[...] = wide_s[...].astype(BF16)
    band_c[...] = wide_c[...].astype(BF16)
    packed[...] = jnp.zeros(packed.shape, F32)
    loads[3].wait()
    st_c[...] = raw_c[...].astype(F32)
    for z in range(HD):
        for y in range(HR):
            cp[z + 1, y + 1] = st_c[pl.ds(z * HR + y, C2, stride=HD * HR), :].astype(BF16)
    chalo.start()

    def block(buf, z, y, n):
        return buf[z, pl.ds(y, n)].reshape(n * buf.shape[2], buf.shape[3])

    def fine_band(z, y0):
        four = dot(
            band_f[...], jnp.concatenate([block(vp, z + a, y0, 6) for a in range(3)], axis=0)
        )
        for r in range(4):
            fine_cell(z, y0 + r, four[r * C1 : (r + 1) * C1])

    def fine_row(z, y):
        fine_cell(z, y, dot(wf, taps(vp, z, y)))

    def fine_cell(z, y, pre):
        s = jax.nn.sigmoid(pre)
        out = (vp[z + 1, y + 1, mid, :].astype(F32) + pre * s).astype(BF16)
        g1[z, y] = s * (1.0 + pre * (1.0 - s))
        fob[z, y] = out

    @pl.loop(1, D - 1)
    def _(z):
        for y in range(1, R - 1):
            fine_row(z, y)

    pool_row = lax.broadcasted_iota(jnp.int32, (W, HW), 0)
    pool_col = lax.broadcasted_iota(jnp.int32, (W, HW), 1)
    pool_mat = (lax.div(pool_row, 2) == pool_col).astype(F32).astype(BF16)
    up_row = lax.broadcasted_iota(jnp.int32, (HW, 3 * W), 0)
    up_col = lax.broadcasted_iota(jnp.int32, (HW, 3 * W), 1)
    up_mat = (
        up_row == lax.div(lax.rem(up_col, W), 2) + 1 - lax.div(up_col, W)
    ).astype(F32).astype(BF16)
    loads[4].wait()
    for t in range(2):
        st_f[t] = raw_f[:, t * 128 : (t + 1) * 128].astype(F32)
    vhalo.wait_recv((6, 7))

    @pl.loop(0, D)
    def _(z):
        for y in (0, R + 1):
            put_shifts(vp, z + 1, y, 1)

    late = (zi == 0).astype(jnp.int32)
    for side in (late, 1 - late):

        @pl.when(side == 0)
        def _():
            vhalo.wait_recv((2, 3, 5))

        @pl.when(side == 1)
        def _():
            vhalo.wait_recv((0, 1, 4))

        for y in range(R + 2):
            put_shifts(vp, side * (D + 1), y, 1)
        for y in (0, 4):
            fine_band(side * (D - 1), y)
        for y in (0, R - 1):
            fine_row(side + 1, y)
        for yc in range(HR):
            four = fob[pl.ds(side * 2, 2), pl.ds(yc * 2, 2)].reshape(4 * C1, W)
            half = dot(four, pool_mat)
            total = half[0:16] + half[16:32] + half[32:48] + half[48:64]
            qp[side + 2, yc + 2, mid, :] = (total * 0.125).astype(BF16)
        qhalo.start(side)

    hear_ring()
    own_shifts(qp, 2, HD, HR, 1)

    def rows_out(rows, store):
        @pl.loop(0, D)
        def _(z):
            for y in range(R):
                value = rows[z, y].astype(F32)
                for t in range(2):
                    store[t, pl.ds(z * R + y, C1, stride=D * R), :] = value[
                        :, t * 128 : (t + 1) * 128
                    ]

    rows_out(fob, st_o)
    for t in range(2):
        fo_ref[:, t * 128 : (t + 1) * 128] = st_o[t].astype(BF16)
    chalo.wait_recv()
    qhalo.wait_recv((6, 7))

    @pl.loop(0, HD)
    def _(z):
        for y in (0, 1, HR + 2, HR + 3):
            put_shifts(qp, z + 2, y, 1)

    for zp in (late, 1 - late):

        @pl.when(zp == 0)
        def _():
            qhalo.wait_recv((2, 3, 5))

        @pl.when(zp == 1)
        def _():
            qhalo.wait_recv((0, 1, 4))

        for k in range(2):
            for y in range(HR + 4):
                put_shifts(qp, zp * 4 + k, y, 1)
        for y0 in range(0, HR + 2, 2):
            two = [
                jnp.concatenate([block(qp, zp * 2 + k + a, y0, 4) for a in range(3)], axis=0)
                for k in range(2)
            ]
            pair = dot(band_c[...], jnp.concatenate(two, axis=1))
            for r in range(2):
                for k in range(2):
                    z, y = zp * 2 + k, y0 + r
                    pre = pair[r * C2 : (r + 1) * C2, k * HW : (k + 1) * HW]
                    s = jax.nn.sigmoid(pre)
                    slope = cp[z, y].astype(F32) * (s * (1.0 + pre * (1.0 - s)))
                    csb[z, y] = slope.astype(BF16)
                    if 1 <= y <= HR:
                        cob[z, y - 1] = (pre * s).astype(BF16)
        for k in range(2):
            z = zp * 2 + k
            wide = dot(csb[z].reshape((HR + 2) * C2, HW), up_mat).astype(BF16)
            for c in range(3):
                tp[z, :, pl.ds(c * C2, C2), :] = wide[:, c * W : (c + 1) * W].reshape(
                    HR + 2, C2, W
                )

    hear_across()

    def turned(rows):
        rows = jnp.concatenate([rows, jnp.zeros((80, rows.shape[1]), F32)], axis=0)
        return jnp.transpose(rows)

    cells = [(z + 1, y + 1) for z in range(HD) for y in range(HR)]
    ck = dot_nt(
        jnp.concatenate([taps(qp, *at) for at in cells], axis=1),
        jnp.concatenate([csb[at] for at in cells], axis=1),
    )
    ck = turned(ck)
    for i in range(4):
        for t in range(4):
            ct[i * 4 + t] = ck[i * 8 : (i + 1) * 8, t * 128 : (t + 1) * 128]
    c_sum.start_scatter()

    @pl.loop(0, HD)
    def _(zc):
        four = dot(
            band_s[...], jnp.concatenate([block(tp, zc + 2 - a, 0, 6) for a in range(3)], axis=0)
        )
        for yc in range(HR):
            spread = four[yc * C1 : (yc + 1) * C1] * 0.125
            for zz in range(2):
                for yy in range(2):
                    z, y = zc * 2 + zz, yc * 2 + yy
                    cot = jnp.concatenate(
                        [st_f[t, pl.ds(z * R + y, C1, stride=D * R), :] for t in range(2)], axis=1
                    )
                    grad = cot + spread
                    fg[z, y] = grad
                    sp[z + 1, y + 1, mid, :] = (grad * g1[z, y]).astype(BF16)

    shalo.start()

    def slope_rows(z, yb):
        if not 0 <= z < D:
            return jnp.zeros((4 * C1, W), BF16)
        return sp[z + 1, pl.ds(yb * 4 + 1, 4), mid, :].reshape(4 * C1, W)

    steps = [(z, yb) for z in range(D + 2) for yb in range(2)]
    pairs = dot_nt(
        jnp.concatenate([block(vp, z, yb * 4, 6) for z, yb in steps], axis=1),
        jnp.concatenate(
            [
                jnp.concatenate([slope_rows(z - a, yb) for a in range(3)], axis=0)
                for z, yb in steps
            ],
            axis=1,
        ),
    )
    pairs = jnp.concatenate([pairs, jnp.zeros((288, 64), F32)], axis=1)
    pairs = jnp.transpose(jnp.concatenate([pairs, jnp.zeros((96, 256), F32)], axis=0))
    for a in range(3):
        total = pairs[a * 64 : a * 64 + 16, 0:144]
        for y in range(1, 4):
            total = total + pairs[a * 64 + y * 16 : a * 64 + y * 16 + 16, y * 48 : y * 48 + 144]
        packed[:, a * 144 : (a + 1) * 144] = total
    fk = packed[...]
    for i in range(2):
        for t in range(4):
            ft[i * 4 + t] = fk[i * 8 : (i + 1) * 8, t * 128 : (t + 1) * 128]
    f_sum.start_scatter()
    c_sum.start_exchange()
    own_shifts(sp, 1, D, R, -1)
    f_sum.start_exchange()
    c_sum.start_gather()
    f_sum.start_gather()
    shalo.wait_recv()
    halo_shifts(sp, 1, D, R, -1)

    @pl.loop(0, D)
    def _(z):
        for y0 in (0, 4):
            four = dot(
                band_t[...],
                jnp.concatenate([block(sp, z + 2 - a, y0, 6) for a in range(3)], axis=0),
            )
            for r in range(4):
                fg[z, y0 + r] = fg[z, y0 + r] + four[r * C1 : (r + 1) * C1]

    rows_out(fg, st_o)
    for t in range(2):
        vg_ref[:, t * 128 : (t + 1) * 128] = st_o[t].astype(BF16)
    for z in range(HD):
        for y in range(HR):
            st_co[pl.ds(z * HR + y, C2, stride=HD * HR), :] = cob[z + 1, y].astype(F32)
    co_ref[...] = st_co[...].astype(BF16)
    for one in (vhalo, chalo, qhalo, shalo, c_sum, f_sum):
        one.wait_send()
    c_sum.finish()
    f_sum.finish()


def emit_kernel(fo, co, vg, ffin, cfin, fo_hbm, co_hbm, vg_hbm, fk_hbm, ck_hbm, fk, ck, sem):
    copies = [
        pltpu.make_async_copy(src, dst, sem.at[i])
        for i, (src, dst) in enumerate(
            ((fo, fo_hbm), (vg, vg_hbm), (co, co_hbm), (fk, fk_hbm), (ck, ck_hbm))
        )
    ]
    for i in range(3):
        copies[i].start()
    for i in range(2):
        for t in range(4):
            tile = ffin[i * 4 + t] * (1048576.0**-0.5)
            for k in range(8):
                tap = t * 8 + k
                if tap < 27:
                    fk[tap, pl.ds(i * 8, 8), :] = tile[:, k * C1 : (k + 1) * C1]
    copies[3].start()
    for t in range(4):
        rows = jnp.concatenate([cfin[i * 4 + t] for i in range(4)], axis=0)
        cols = jnp.transpose(rows * (131072.0**-0.5))
        for k in range(8):
            tap = t * 8 + k
            if tap < 27:
                ck[tap] = cols[k * C1 : (k + 1) * C1, :]
    copies[4].start()
    for one in copies:
        one.wait()


def local(volume, fine_kernel, coarse_kernel, fine_cotangent, coarse_cotangent):
    kf = fine_kernel.reshape(27 * C1, C1)
    kc = coarse_kernel.transpose(0, 1, 2, 4, 3).reshape(27 * C1, C2)
    hbm = pl.BlockSpec(memory_space=pltpu.HBM)
    vmem = pl.BlockSpec(memory_space=pltpu.VMEM)
    dma = pltpu.SemaphoreType.DMA
    V = pltpu.VMEM
    tile = (8, 128)
    fine, coarse = (C1 * D * R, W), (C2 * HD * HR, HW)
    parts = pl.pallas_call(
        kernel,
        out_shape=[
            jax.ShapeDtypeStruct(fine, BF16),
            jax.ShapeDtypeStruct(coarse, BF16),
            jax.ShapeDtypeStruct(fine, BF16),
            jax.ShapeDtypeStruct((8, *tile), F32),
            jax.ShapeDtypeStruct((16, *tile), F32),
        ],
        in_specs=[hbm] * 5,
        out_specs=[vmem] * 5,
        scratch_shapes=[
            V(fine, BF16), V(fine, BF16), V(coarse, BF16),
            V((27 * C1, C1), BF16), V((27 * C1, C2), BF16),
            V((2, C1 * D * R, 128), F32), V((2, C1 * D * R, 128), F32), V(coarse, F32),
            V((2, C1 * D * R, 128), F32), V(coarse, F32),
            V((D + 2, R + 2, 3 * C1, W), BF16),
            V((HD + 2, HR + 2, C2, HW), BF16),
            V((HD + 4, HR + 4, 3 * C1, HW), BF16),
            V((HD + 2, HR + 2, 3 * C2, W), BF16),
            V((D + 2, R + 2, 3 * C1, W), BF16),
            V((D, R, C1, W), BF16), V((D, R, C1, W), F32), V((D, R, C1, W), F32),
            V((HD + 2, HR + 2, C2, HW), BF16), V((HD + 2, HR, C2, HW), BF16),
            V((C1, 27 * C1), F32), V((C1, 27 * C2), F32),
            V((C1, 27 * C1), F32), V((C2, 27 * C1), F32), V((C1, 512), F32),
            V((64, 864), F32), V((64, 864), F32), V((64, 1728), F32), V((64, 576), F32),
            V((64, 864), BF16), V((64, 864), BF16), V((64, 1728), BF16), V((64, 576), BF16),
            V((8, *tile), F32), V((16, *tile), F32),
            V((8, *tile), F32), V((16, *tile), F32),
            V((16, *tile), F32), V((8, *tile), F32),
            dma((5,)), dma((4, 8)), dma((4, 8)), dma((2, 8)), dma((2, 8)), pltpu.SemaphoreType.REGULAR((3,)),
            dma((8,)), dma((8,)), dma((16,)), dma((16,)), dma((8,)), dma((8,)),
            dma((16,)), dma((16,)), dma((8,)), dma((8,)), dma((16,)), dma((16,)),
        ],
        compiler_params=pltpu.CompilerParams(
            collective_id=0, has_side_effects=True, vmem_limit_bytes=48 << 20
        ),
        name="unet_levels",
    )(
        *(
            pltpu.with_memory_space_constraint(value, pltpu.HBM)
            for value in (
                volume.reshape(fine), fine_cotangent.reshape(fine),
                coarse_cotangent.reshape(coarse), kf, kc,
            )
        )
    )
    fo, co, vg, fk, ck = pl.pallas_call(
        emit_kernel,
        out_shape=[
            jax.ShapeDtypeStruct(fine, BF16),
            jax.ShapeDtypeStruct(coarse, BF16),
            jax.ShapeDtypeStruct(fine, BF16),
            jax.ShapeDtypeStruct((27, C1, C1), F32),
            jax.ShapeDtypeStruct((27, C1, C2), F32),
        ],
        in_specs=[vmem] * 5,
        out_specs=[hbm] * 5,
        scratch_shapes=[V((27, C1, C1), F32), V((27, C1, C2), F32), dma((5,))],
        compiler_params=pltpu.CompilerParams(vmem_limit_bytes=8 << 20),
        name="emit",
    )(*parts)
    return (
        fo.reshape(volume.shape),
        co.reshape(coarse_cotangent.shape),
        vg.reshape(volume.shape),
        fk.reshape(fine_kernel.shape),
        ck.reshape(3, 3, 3, C1, C2).transpose(0, 1, 2, 4, 3),
    )


def solution(mesh):
    block = P(None, "gx", "gy", None)
    return jax.shard_map(
        local,
        mesh=mesh,
        in_specs=(block, P(), P(), block, block),
        out_specs=(block, block, block, P(), P()),
        check_vma=False,
    )
```
